128 devices in a mesh: head: 4 (over y), blk: 32 (over x, z, core).
Axes of the slice: x: 4, y: 4, z: 4, core: 2. Of those that a mesh axis runs over, the one named last changes fastest.
Arguments:
- hidden_in: bfloat16 [12288, 1408], P('blk'), may hold values from -25 to 25
- queries: bfloat16 [12288, 1408], P('blk', 'head'), may hold values from -7.182936 to 7.182936
- keys: bfloat16 [12288, 1408], P('blk', 'head'), may hold values from -7.182936 to 7.182936
- values: bfloat16 [12288, 1408], P('blk', 'head'), may hold values from -10 to 10
- out_weight: bfloat16 [1408, 1408], P('head'), may hold values from -0.15625 to 0.15625
- out_bias: float32 [1408], replicated, may hold values from -3 to 3
- norm_gain: float32 [1408], replicated, may hold values from 0.1 to 1.9
- norm_bias: float32 [1408], replicated, may hold values from -3 to 3
- up_weight: bfloat16 [1408, 6144], P(None, 'head'), may hold values from -0.15625 to 0.15625
- up_bias: float32 [6144], P('head'), may hold values from -3 to 3
- down_weight: bfloat16 [6144, 1408], P('head'), may hold values from -0.078125 to 0.078125
- down_bias: float32 [1408], replicated, may hold values from -3 to 3
- merge_weight: bfloat16 [5632, 4096], P(None, 'head'), may hold values from -0.078125 to 0.078125
- merge_bias: float32 [4096], P('head'), may hold values from -3 to 3
- group_segments: int32 [3072], P('blk'), may hold values from 0 to 63, never falling along the last dimension, each value on 1 to 2304 neighbouring positions
- owner_slots: int32 [64], replicated, may hold values from 0 to 63, each once
Outputs:
- merged_out: bfloat16 [3072, 4096], P('blk', 'head')
- state_rms: float32 [64], P('blk')
- logit_max: float32 [64, 16], P('blk', 'head')
The draws below stay inside these ranges and needn't reach their ends.
Inputs may be any that keep to these rules, and one draw needn't show every extreme that they name: `group_segments`: request numbers never fall along the groups; every request number is used, each by 1 to 2304 groups, and one request has exactly 2304 groups. `owner_slots`: each slot number appears once.
All inputs are finite; a program needn't handle non-finite values.
Results may differ from the reference program's by a relative error of at most 0.013.
Values may be sent and summed in bfloat16 or wider, within the bound.
No kernel may reach another device: no remote copies, remote signals or barrier semaphores. Data moves between devices by JAX's collectives and lax.ppermute only.
A program may use at most 128 MiB of HBM per device.

```python
import math
import jax
import jax.numpy as jnp
import numpy as np
from jax import lax

D = 1408
HEADS = 16
HD = 88
FF = 6144
OUTW = 4096
TOKENS = 12288
GROUPS = 3072
REQ = 64
CLIP = 2304


def draw_queries(key, part):
    sampled = jnp.clip(1.4 * jax.random.normal(jax.random.fold_in(key, 1), (TOKENS, D), jnp.float32), -6.0, 6.0)
    return sampled.astype(jnp.bfloat16)


def draw_keys(key, part):
    sampled = jnp.clip(1.4 * jax.random.normal(jax.random.fold_in(key, 2), (TOKENS, D), jnp.float32), -6.0, 6.0)
    return sampled.astype(jnp.bfloat16)


def draw_hidden_in(key, part):
    positions = jnp.arange(TOKENS).astype(jnp.float32)
    row_ramp = 1.0 + 2.0 * positions / (TOKENS - 1)
    sampled = jnp.clip(jax.random.normal(jax.random.fold_in(key, 3), (TOKENS, D), jnp.float32), -6.0, 6.0) * row_ramp[:, None]
    return sampled.astype(jnp.bfloat16)


def shard_levels(stream_key, extent, shards, smallest, top_value):
    factor_of = 1.0
    for axis_at, blocks in shards:
        draws = jax.random.uniform(jax.random.fold_in(jax.random.fold_in(stream_key, 6), axis_at), (blocks,), jnp.float32, smallest / len(shards), top_value / len(shards))
        factor_of = factor_of * jnp.repeat(jnp.exp(draws), extent[axis_at] // blocks).reshape((-1,) + (1,) * (len(extent) - 1 - axis_at))
    return factor_of


def length_profile(number_of, total, reach, slope):
    weights = [(1 << 20) // math.isqrt(rank ** slope) + 1 for rank in range(2, number_of + 1)]
    surplus, given = total - reach - (number_of - 1), [1] * (number_of - 1)
    while surplus > 0:
        free = [i for i in range(number_of - 1) if given[i] < reach]
        pool, remaining = sum([weights[i] for i in free]), surplus
        for i in free:
            more = min(reach - given[i], max(1, remaining * weights[i] // pool), surplus)
            given[i] = given[i] + more
            surplus = surplus - more
    return np.array([reach] + given)


def uneven_parts(stream_key, count, total, reach, skew):
    if count == 2:
        one = jax.random.randint(stream_key, (), max(1, total - reach), min(reach, total - 1) + 1)
        return jnp.stack([one, total - one])
    tallies = jnp.asarray(length_profile(count, total, reach, skew), jnp.int32)
    couples = (count - 1) // 2
    source_of, taker = tallies[1:1 + 2 * couples:2], tallies[2:2 + 2 * couples:2]
    slack = jnp.minimum(source_of - 1, reach - taker)
    passed = jax.random.randint(jax.random.fold_in(stream_key, 1), (couples,), 0, 1 << 20) % (slack + 1)
    tallies = tallies.at[1:1 + 2 * couples:2].set(source_of - passed).at[2:2 + 2 * couples:2].set(taker + passed)
    return tallies[jax.random.permutation(jax.random.fold_in(stream_key, 2), count)]


def noise(rng, shape, spread, limit, shards=(), held_as=jnp.bfloat16):
    level = shard_levels(rng, shape, shards, -0.22, 0.18) if shards else 1.0
    drawn = jax.random.normal(rng, shape, jnp.float32) * spread * level
    return jnp.minimum(jnp.maximum(drawn, -limit), limit).astype(held_as)


def setup_inputs(seed: int = 0) -> dict:
    streams_of = jax.random.split(jax.random.key(seed), 17)
    hidden_in = draw_hidden_in(jax.random.fold_in(streams_of[16], 71), 0)
    queries = draw_queries(jax.random.fold_in(streams_of[16], 71), 0)
    keys = draw_keys(jax.random.fold_in(streams_of[16], 71), 0)
    values = noise(streams_of[3], (TOKENS, D), 2.0, 10.0, ((0, 32), (1, 4)))
    out_weight = noise(streams_of[4], (D, D), D ** -0.5, 0.15625, ((0, 4),))
    out_bias = noise(streams_of[5], (D,), 0.5, 3.0, (), jnp.float32)
    norm_gain = jnp.clip(1.0 + 0.18 * jax.random.normal(streams_of[6], (D,), jnp.float32), 0.1, 1.9)
    norm_bias = noise(streams_of[7], (D,), 0.5, 3.0, (), jnp.float32)
    up_weight = noise(streams_of[8], (D, FF), D ** -0.5, 0.15625, ((1, 4),))
    up_bias = noise(streams_of[9], (FF,), 0.5, 3.0, ((0, 4),), jnp.float32)
    down_weight = noise(streams_of[10], (FF, D), FF ** -0.5, 0.078125, ((0, 4),))
    down_bias = noise(streams_of[11], (D,), 0.5, 3.0, (), jnp.float32)
    merge_weight = noise(streams_of[12], (4 * D, OUTW), (4 * D) ** -0.5, 0.078125, ((1, 4),))
    merge_bias = noise(streams_of[13], (OUTW,), 0.5, 3.0, ((0, 4),), jnp.float32)
    group_segments = jnp.searchsorted(jnp.cumsum(uneven_parts(streams_of[14], REQ, GROUPS, CLIP, 2)), jnp.arange(GROUPS), side="right").astype(jnp.int32)
    owner_slots = jax.random.permutation(streams_of[15], REQ).astype(jnp.int32)
    return {"hidden_in": hidden_in, "queries": queries, "keys": keys, "values": values, "out_weight": out_weight, "out_bias": out_bias, "norm_gain": norm_gain, "norm_bias": norm_bias, "up_weight": up_weight, "up_bias": up_bias, "down_weight": down_weight, "down_bias": down_bias, "merge_weight": merge_weight, "merge_bias": merge_bias, "group_segments": group_segments, "owner_slots": owner_slots}


NEGATIVE = -1e+30
EPSILON = 1e-06

def reference(hidden_in, queries, keys, values, out_weight, out_bias, norm_gain, norm_bias, up_weight, up_bias, down_weight, down_bias, merge_weight, merge_bias, group_segments, owner_slots):
    row_segments = jnp.repeat(group_segments, 4)
    query_heads = queries.astype(jnp.float32).reshape(TOKENS, HEADS, HD)
    key_heads = keys.astype(jnp.float32).reshape(TOKENS, HEADS, HD)
    value_heads = values.astype(jnp.float32).reshape(TOKENS, HEADS, HD)
    score_scale = HD ** (-0.5)
    query_block = math.gcd(TOKENS, 256)

    def attend_block(block_start):
        block_queries = lax.dynamic_slice_in_dim(query_heads, block_start, query_block, 0)
        block_segments = lax.dynamic_slice_in_dim(row_segments, block_start, query_block, 0)
        scores = jnp.einsum('qhd,khd->hqk', block_queries, key_heads) * score_scale
        allowed = (block_segments[:, None] == row_segments[None, :])[None]
        scores = jnp.where(allowed, scores, NEGATIVE)
        block_max = lax.optimization_barrier(jnp.max(scores, axis=-1))
        exponents = jnp.where(allowed, jnp.exp(scores - block_max[..., None]), 0.0)
        totals = lax.optimization_barrier(jnp.sum(exponents, axis=-1))
        weights = lax.optimization_barrier(exponents.astype(jnp.bfloat16))
        numerators = jnp.einsum('hqk,khd->hqd', weights.astype(jnp.float32), value_heads)
        attended = (numerators / totals[..., None]).astype(jnp.bfloat16)
        return (jnp.transpose(attended, (1, 0, 2)).reshape(query_block, D), jnp.transpose(block_max))
    starts = (jnp.arange(TOKENS // query_block) * query_block).astype(jnp.int32)
    attended, row_max = lax.map(attend_block, starts)
    attended = attended.reshape(TOKENS, D)
    row_max = row_max.reshape(TOKENS, HEADS)
    mixed = hidden_in.astype(jnp.float32) + jnp.dot(attended, out_weight, preferred_element_type=jnp.float32) + out_bias
    row_mean = lax.optimization_barrier(jnp.mean(mixed, axis=-1, keepdims=True))
    centered = mixed - row_mean
    row_var = lax.optimization_barrier(jnp.mean(centered * centered, axis=-1, keepdims=True))
    normed = (centered * lax.rsqrt(row_var + EPSILON) * norm_gain + norm_bias).astype(jnp.bfloat16)
    up_proj = jnp.dot(normed, up_weight, preferred_element_type=jnp.float32) + up_bias
    hidden_units = jax.nn.gelu(up_proj, approximate=False).astype(jnp.bfloat16)
    state = mixed + jnp.dot(hidden_units, down_weight, preferred_element_type=jnp.float32) + down_bias
    state_bf = state.astype(jnp.bfloat16)
    merged_out = (jnp.dot(state_bf.reshape(GROUPS, 4 * D), merge_weight, preferred_element_type=jnp.float32) + merge_bias).astype(jnp.bfloat16)
    member = row_segments[None, :] == jnp.arange(REQ, dtype=jnp.int32)[:, None]
    squares = lax.optimization_barrier(jnp.sum(state * state, axis=-1))
    request_sums = lax.optimization_barrier(jnp.sum(jnp.where(member, squares[None, :], 0.0), axis=-1))
    counts = lax.optimization_barrier(jnp.sum(member.astype(jnp.float32), axis=-1))
    request_rms = jnp.sqrt(request_sums / (counts * D) + EPSILON)
    request_max = lax.optimization_barrier(jnp.max(jnp.where(member[:, :, None], row_max[None], NEGATIVE), axis=1))
    state_rms = jnp.zeros((REQ,), jnp.float32).at[owner_slots].set(request_rms)
    logit_max = jnp.zeros((REQ, HEADS), jnp.float32).at[owner_slots].set(request_max)
    return (merged_out, state_rms, logit_max)
```

```python
import functools

import jax
import jax.numpy as jnp
import numpy as np
from jax import lax
from jax.experimental import pallas as pl
from jax.experimental.pallas import tpu as pltpu
from jax.sharding import Mesh
from jax.sharding import PartitionSpec as P

HD = 88
NEGATIVE = -1e30
EPSILON = 1e-06
F32 = jnp.float32
BF16 = jnp.bfloat16

NY, NX, NZ, NC = 4, 4, 4, 2
ROWS = 384
CHUNKS = NX * NZ * NC
EXP2_SCALE = float(np.log2(np.e) / np.sqrt(HD))


def ring(size, shift):
    return [(i, (i + shift) % size) for i in range(size)]


def shifted(value, axis, size):
    order = [1, size - 1] + list(range(2, size - 1)) if size > 2 else [1]
    got = {k: lax.ppermute(value, axis, ring(size, k)) for k in order}
    return [got[k] for k in range(1, size)]


def params(mib):
    return pltpu.CompilerParams(vmem_limit_bytes=mib << 20)


def attention_kernel(table, qt_ref, start_ref, end_ref, *rest):
    keys_in, values_in = rest[:8], rest[8:16]
    out_ref, max_ref = rest[16], rest[17]
    keys, values, s0, s1, p0, p1, total, sems = rest[18:]
    part = pl.program_id(0)
    low, high = table[0, part], table[1, part]
    start_last, end_first = table[2, part], table[3, part]
    z_here, c_here = table[4, 0], table[4, 1]

    @pl.when(part == 0)
    def _():
        copies = []
        for i in range(8):
            copies.append(pltpu.make_async_copy(keys_in[i], keys.at[i], sems.at[i]))
            copies.append(pltpu.make_async_copy(values_in[i], values.at[i], sems.at[8 + i]))
        for copy in copies:
            copy.start()
        for copy in copies:
            copy.wait()

    def place(chunk):
        z_of, c_of = (chunk >> 1) & 3, chunk & 1
        piece = ((z_here - z_of) & 3) * 2 + (c_here ^ c_of)
        return piece, chunk >> 3

    queries = qt_ref[0]

    def score(chunk, scores):
        piece, at = place(chunk)
        scores[...] = jnp.dot(keys[piece, at], queries, preferred_element_type=F32)

    def gather(chunk, weights, factor):
        piece, at = place(chunk)
        total[...] = total[...] * factor + jnp.dot(
            values[piece, at], weights[...], preferred_element_type=F32
        )

    def soften(chunk, scores, weights, top, mass, masked):
        s = scores[...]
        if masked:
            row = chunk * ROWS + lax.broadcasted_iota(jnp.int32, s.shape, 0)
            s = jnp.where((row >= start_ref[0]) & (row < end_ref[0]), s, NEGATIVE)
        new_top = jnp.maximum(top, jnp.max(s, axis=0, keepdims=True))
        exponents = jnp.exp2((s - new_top) * EXP2_SCALE)
        factor = jnp.exp2((top - new_top) * EXP2_SCALE)
        weights[...] = exponents.astype(BF16)
        return new_top, mass * factor + jnp.sum(exponents, axis=0, keepdims=True), factor

    total[...] = jnp.zeros_like(total)
    p1[...] = jnp.zeros_like(p1)
    low_pair, high_pair = low // 2, (high + 1) // 2
    score(2 * low_pair, s0)

    def step(pair, carried, masked):
        top, mass, factor = carried
        chunk = 2 * pair
        score(chunk + 1, s1)
        gather(jnp.maximum(chunk - 1, 0), p1, factor)
        top, mass, factor = soften(chunk, s0, p0, top, mass, masked)
        score(jnp.minimum(chunk + 2, CHUNKS - 1), s0)
        gather(chunk, p0, factor)
        return soften(chunk + 1, s1, p1, top, mass, masked)

    def one_pair(pair, carried):
        full = (start_last <= 2 * pair * ROWS) & (end_first >= (2 * pair + 2) * ROWS)
        return lax.cond(
            full, lambda c: step(pair, c, False), lambda c: step(pair, c, True), carried
        )

    first = (
        jnp.full((1, ROWS), NEGATIVE, F32),
        jnp.zeros((1, ROWS), F32),
        jnp.ones((1, ROWS), F32),
    )
    top, mass, factor = lax.fori_loop(low_pair, high_pair, one_pair, first)
    gather(2 * high_pair - 1, p1, factor)
    attended = jnp.transpose(total[...] / mass).astype(BF16)
    for y in range(NY):
        out_ref[y, 0] = attended[y * 96 : (y + 1) * 96]
    max_ref[0] = top


def attention(table, queries, starts, ends, key_pieces, value_pieces):
    whole = pl.BlockSpec(memory_space=pl.ANY)
    row = pl.BlockSpec((1, 1, ROWS), lambda i, t: (i, 0, 0))
    return pl.pallas_call(
        attention_kernel,
        out_shape=(
            jax.ShapeDtypeStruct((NY, NX, ROWS // NY, HD), BF16),
            jax.ShapeDtypeStruct((NX, 1, ROWS), F32),
        ),
        grid_spec=pltpu.PrefetchScalarGridSpec(
            num_scalar_prefetch=1,
            grid=(NX,),
            in_specs=[pl.BlockSpec((1, HD, ROWS), lambda i, t: (i, 0, 0)), row, row] + [whole] * 16,
            out_specs=(
                pl.BlockSpec((NY, 1, ROWS // NY, HD), lambda i, t: (0, i, 0, 0)),
                row,
            ),
            scratch_shapes=[
                pltpu.VMEM((8, NX, ROWS, HD), BF16),
                pltpu.VMEM((8, NX, HD, ROWS), BF16),
                pltpu.VMEM((ROWS, ROWS), F32),
                pltpu.VMEM((ROWS, ROWS), F32),
                pltpu.VMEM((ROWS, ROWS), BF16),
                pltpu.VMEM((ROWS, ROWS), BF16),
                pltpu.VMEM((HD, ROWS), F32),
                pltpu.SemaphoreType.DMA((16,)),
            ],
        ),
        compiler_params=params(40),
        name="attention",
    )(table, queries, starts, ends, *key_pieces, *value_pieces)


def project_kernel(y_ref, att_ref, w0, w1, w2, w3, hidden_ref, bias_ref, gain_ref, shift_ref,
                   mixed_ref, normed_ref):
    y = y_ref[0]
    mixed = hidden_ref[...].astype(F32) + bias_ref[...]
    for k, w_ref in enumerate((w0, w1, w2, w3)):
        base = ((y - k) & 3) * 4
        for i in range(4):
            mixed = mixed + jnp.dot(att_ref[base + i], w_ref[i], preferred_element_type=F32)
    mixed_ref[...] = mixed
    mean = jnp.mean(mixed, axis=-1, keepdims=True)
    centered = mixed - mean
    var = jnp.mean(centered * centered, axis=-1, keepdims=True)
    normed = centered * lax.rsqrt(var + EPSILON) * gain_ref[...] + shift_ref[...]
    normed_ref[...] = normed.astype(BF16)


def project(y, attended, weights, hidden, bias, gain, shift):
    rows, width = ROWS // NY, hidden.shape[1]
    full = lambda *shape: pl.BlockSpec(shape, lambda i, t: (0,) * len(shape))
    return pl.pallas_call(
        project_kernel,
        out_shape=(
            jax.ShapeDtypeStruct((rows, width), F32),
            jax.ShapeDtypeStruct((rows, width), BF16),
        ),
        grid_spec=pltpu.PrefetchScalarGridSpec(
            num_scalar_prefetch=1,
            grid=(1,),
            in_specs=[full(16, rows, HD)]
            + [full(4, HD, width)] * 4
            + [pl.BlockSpec((rows, width), lambda i, t: (t[0], 0))]
            + [full(1, width)] * 3,
            out_specs=(full(rows, width), full(rows, width)),
        ),
        compiler_params=params(40),
        name="project",
    )(y, attended, *weights, hidden, bias, gain, shift)


def mlp_kernel(x0, x1, x2, x3, up_ref, bias_ref, down_ref, o0, o1, o2, o3, rows, total):
    step = pl.program_id(0)
    size = ROWS // NY

    @pl.when(step == 0)
    def _():
        for k, x in enumerate((x0, x1, x2, x3)):
            rows[k * size : (k + 1) * size] = x[...]

    units = jnp.dot(rows[...], up_ref[...], preferred_element_type=F32) + bias_ref[...]
    units = 0.5 * units * (1.0 + lax.erf(units * float(np.sqrt(0.5))))
    part = jnp.dot(units.astype(BF16), down_ref[...], preferred_element_type=F32)

    @pl.when(step == 0)
    def _():
        total[...] = part

    @pl.when(step > 0)
    def _():
        total[...] += part

    @pl.when(step == pl.num_programs(0) - 1)
    def _():
        for k, o in enumerate((o0, o1, o2, o3)):
            o[...] = total[k * size : (k + 1) * size].astype(o.dtype)


def mlp(pieces, up_weight, up_bias, down_weight):
    size, width = ROWS // NY, up_weight.shape[0]
    hidden = up_weight.shape[1]
    block = 384
    piece = pl.BlockSpec((size, width), lambda i: (0, 0))
    return pl.pallas_call(
        mlp_kernel,
        out_shape=[jax.ShapeDtypeStruct((size, width), F32 if k == 0 else BF16) for k in range(NY)],
        grid=(hidden // block,),
        in_specs=[piece] * 4
        + [
            pl.BlockSpec((width, block), lambda i: (0, i)),
            pl.BlockSpec((1, block), lambda i: (0, i)),
            pl.BlockSpec((block, width), lambda i: (i, 0)),
        ],
        out_specs=[piece] * 4,
        scratch_shapes=[pltpu.VMEM((ROWS, width), BF16), pltpu.VMEM((ROWS, width), F32)],
        compiler_params=params(40),
        name="mlp",
    )(*pieces, up_weight, up_bias, down_weight)


def merge_kernel(y_ref, x0, x1, x2, x3, weight_ref, bias_ref, out_ref, rows, total):
    step = pl.program_id(0)
    size = ROWS // NY
    groups = ROWS // 4

    @pl.when(step == 0)
    def _():
        for k, x in enumerate((x0, x1, x2, x3)):
            rows[k * size : (k + 1) * size] = x[...]

    at = lax.broadcasted_iota(jnp.int32, (groups, ROWS), 1)
    group = lax.broadcasted_iota(jnp.int32, (groups, ROWS), 0)
    piece = (at >= size).astype(jnp.int32) + (at >= 2 * size) + (at >= 3 * size)
    row = ((y_ref[0] - piece) & 3) * size + at - piece * size
    pick = (row == 4 * group + step).astype(F32).astype(BF16)
    chosen = jnp.dot(pick, rows[...], preferred_element_type=F32).astype(BF16)
    part = jnp.dot(chosen, weight_ref[...], preferred_element_type=F32)

    @pl.when(step == 0)
    def _():
        total[...] = part

    @pl.when(step > 0)
    def _():
        total[...] += part

    @pl.when(step == pl.num_programs(0) - 1)
    def _():
        out_ref[...] = (total[...] + bias_ref[...]).astype(BF16)


def merge(y, pieces, weight, bias):
    size, width = pieces[0].shape
    features = weight.shape[1]
    groups = ROWS // 4
    piece = pl.BlockSpec((size, width), lambda i, t: (0, 0))
    return pl.pallas_call(
        merge_kernel,
        out_shape=jax.ShapeDtypeStruct((groups, features), BF16),
        grid_spec=pltpu.PrefetchScalarGridSpec(
            num_scalar_prefetch=1,
            grid=(4,),
            in_specs=[piece] * 4
            + [
                pl.BlockSpec((width, features), lambda i, t: (i, 0)),
                pl.BlockSpec((1, features), lambda i, t: (0, 0)),
            ],
            out_specs=pl.BlockSpec((groups, features), lambda i, t: (0, 0)),
            scratch_shapes=[pltpu.VMEM((ROWS, width), BF16), pltpu.VMEM((groups, features), F32)],
        ),
        compiler_params=params(40),
        name="merge",
    )(y, *pieces, weight, bias)


def body(
    hidden_in,
    queries,
    keys,
    values,
    out_weight,
    out_bias,
    norm_gain,
    norm_bias,
    up_weight,
    up_bias,
    down_weight,
    down_bias,
    merge_weight,
    merge_bias,
    group_segments,
    owner_slots,
):
    heads = 4
    width = hidden_in.shape[1]
    request_total = owner_slots.shape[0]
    x = lax.axis_index("x")
    y = lax.axis_index("y")
    z = lax.axis_index("z")
    c = lax.axis_index("c")
    y_scalar = jnp.reshape(y, (1,)).astype(jnp.int32)

    key_parts = keys.reshape(ROWS, heads, HD).transpose(1, 0, 2)
    value_parts = values.T.reshape(heads, HD, ROWS)
    query_parts = queries.T.reshape(heads, HD, ROWS)
    both_parts = jnp.concatenate([value_parts, query_parts], axis=1)
    key_own = lax.all_to_all(key_parts, "x", 0, 0)
    key_z = [key_own] + shifted(key_own, "z", NZ)
    both_own = lax.all_to_all(both_parts, "x", 0, 0)
    value_own = both_own[:, :HD]
    query_own = both_own[:, HD:]
    value_z = [value_own] + shifted(value_own, "z", NZ)
    swap = [(0, 1), (1, 0)]
    key_pieces, value_pieces = [], []
    for k in range(NZ):
        key_pieces += [key_z[k], lax.ppermute(key_z[k], "c", swap)]
        value_pieces += [value_z[k], lax.ppermute(value_z[k], "c", swap)]

    segments_x = [group_segments] + shifted(group_segments, "x", NX)
    relative = jnp.stack(segments_x)
    group_rows = jnp.take(relative, (x - jnp.arange(NX)) & 3, axis=0)
    requests = jnp.arange(request_total, dtype=jnp.int32)
    counts = jnp.sum((relative.reshape(-1)[None, :] == requests[:, None]).astype(F32), axis=1)
    for axis, size in (("z", NZ), ("c", NC)):
        counts = counts + sum(shifted(counts, axis, size))
    counts = counts * 4.0
    row_segments = jnp.repeat(group_rows, 4, axis=1)
    below = requests[:, None, None] < row_segments[None]
    upto = requests[:, None, None] <= row_segments[None]
    starts = jnp.sum(jnp.where(below, counts[:, None, None], 0.0), axis=0).astype(jnp.int32)
    ends = jnp.sum(jnp.where(upto, counts[:, None, None], 0.0), axis=0).astype(jnp.int32)
    table = jnp.stack(
        [
            starts[:, 0] // ROWS,
            (ends[:, -1] + ROWS - 1) // ROWS,
            starts[:, -1],
            ends[:, 0],
            jnp.stack([z, c, z, c]).astype(jnp.int32),
        ]
    )
    attended, row_max = attention(
        table, query_own, starts[:, None], ends[:, None], key_pieces, value_pieces
    )

    attended = lax.all_to_all(attended.reshape(16, ROWS // NY, HD), ("y", "x"), 0, 0)
    weights = [
        w.reshape(heads, HD, width) for w in [out_weight] + shifted(out_weight, "y", NY)
    ]
    mixed, normed = project(
        y_scalar, attended, weights, hidden_in, out_bias[None], norm_gain[None], norm_bias[None]
    )

    member = row_segments[None] == requests[:, None, None]
    request_max = jnp.max(jnp.where(member, row_max[:, 0][None], NEGATIVE), axis=(1, 2))
    request_max = request_max * (HD**-0.5)
    for axis, size in (("z", NZ), ("c", NC)):
        for other in shifted(request_max, axis, size):
            request_max = jnp.maximum(request_max, other)
    head_max = jnp.stack([request_max] + shifted(request_max, "x", NX))
    head_max = jnp.take(head_max, (x - jnp.arange(NX)) & 3, axis=0)
    slot_ids = (x * (NZ * NC) + z * NC + c) * 2 + jnp.arange(2, dtype=jnp.int32)
    mine = owner_slots[None, :] == slot_ids[:, None]
    logit_max = jnp.max(jnp.where(mine[:, None, :], head_max[None], NEGATIVE), axis=-1)

    normed_all = [normed] + shifted(normed, "y", NY)
    down = mlp(normed_all, up_weight, up_bias[None], down_weight)
    state = mixed + down_bias + down[0]
    for k in range(1, NY):
        back = lax.ppermute(down[k], "y", ring(NY, NY - k))
        state = state + back.astype(F32)
    state_bf = state.astype(BF16)
    merged_out = merge(
        y_scalar, [state_bf] + shifted(state_bf, "y", NY), merge_weight, merge_bias[None]
    )

    squares = jnp.sum(state * state, axis=-1)
    own_groups = lax.dynamic_slice_in_dim(group_segments, y * (ROWS // 16), ROWS // 16)
    own_rows = jnp.repeat(own_groups, 4)
    sums = jnp.sum(jnp.where(own_rows[None] == requests[:, None], squares[None], 0.0), axis=1)
    for axis, size in (("y", NY), ("x", NX), ("z", NZ), ("c", NC)):
        sums = sums + sum(shifted(sums, axis, size))
    rms = jnp.sqrt(sums / (counts * width) + EPSILON)
    state_rms = jnp.sum(jnp.where(mine, rms[None], 0.0), axis=-1)
    return (merged_out, state_rms, logit_max)


def solution(mesh):
    fine = Mesh(mesh.devices.reshape(NY, NX, NZ, NC), ("y", "x", "z", "c"))
    blk = ("x", "z", "c")
    in_specs = (
        P(blk, None),
        P(blk, "y"),
        P(blk, "y"),
        P(blk, "y"),
        P("y", None),
        P(),
        P(),
        P(),
        P(None, "y"),
        P("y"),
        P("y", None),
        P(),
        P(None, "y"),
        P("y"),
        P(blk),
        P(),
    )
    out_specs = (P(blk, "y"), P(blk), P(blk, "y"))
    return jax.shard_map(body, mesh=fine, in_specs=in_specs, out_specs=out_specs, check_vma=False)
```

```python
import functools

import jax
import jax.numpy as jnp
import numpy as np
from jax import lax
from jax.experimental import pallas as pl
from jax.experimental.pallas import tpu as pltpu
from jax.sharding import Mesh
from jax.sharding import PartitionSpec as P

HD = 88
NEGATIVE = -1e30
EPSILON = 1e-06
F32 = jnp.float32
BF16 = jnp.bfloat16

NY, NX, NZ, NC = 4, 4, 4, 2
ROWS = 384
CHUNKS = NX * NZ * NC
EXP2_SCALE = float(np.log2(np.e) / np.sqrt(HD))


def ring(size, shift):
    return [(i, (i + shift) % size) for i in range(size)]


def shifted(value, axis, size):
    order = [1, size - 1] + list(range(2, size - 1)) if size > 2 else [1]
    got = {k: lax.ppermute(value, axis, ring(size, k)) for k in order}
    return [got[k] for k in range(1, size)]


def in_hbm(value):
    return pltpu.with_memory_space_constraint(value, pltpu.HBM)


def params(mib):
    return pltpu.CompilerParams(vmem_limit_bytes=mib << 20)


def attention_kernel(table, qt_ref, start_ref, end_ref, *rest):
    own, behind, ahead, far_a, far_b, own_c, behind_c, ahead_c, far_a_c, far_b_c = rest[:10]
    out_ref, max_ref = rest[10], rest[11]
    keys, values, s0, s1, p0, p1, total, sems = rest[12:]
    part = pl.program_id(0)
    low, high = table[0, part], table[1, part]
    start_last, end_first = table[2, part], table[3, part]
    z_here, c_here = table[4, 0], table[4, 1]

    @pl.when(part == 0)
    def _():
        copies = []
        for core, pieces in enumerate(
            ((own, behind, far_a, far_b, ahead), (own_c, behind_c, far_a_c, far_b_c, ahead_c))
        ):
            for i, (piece, slot, rows) in enumerate(
                zip(pieces, (0, 1, 2, 2, 3), ((0, 4), (0, 4), (0, 2), (2, 2), (0, 4)))
            ):
                at = pl.ds(*rows)
                for j, target in enumerate((keys, values)):
                    copies.append(
                        pltpu.make_async_copy(
                            piece.at[:, pl.ds(j * HD, HD)],
                            target.at[2 * slot + core, at],
                            sems.at[(core * 5 + i) * 2 + j],
                        )
                    )
        for copy in copies:
            copy.start()
        for copy in copies:
            copy.wait()

    def place(chunk):
        z_of, c_of = (chunk >> 1) & 3, chunk & 1
        piece = ((z_here - z_of) & 3) * 2 + (c_here ^ c_of)
        return piece, chunk >> 3

    queries = qt_ref[0]

    def score(chunk, scores):
        piece, at = place(chunk)
        scores[...] = lax.dot_general(
            keys[piece, at], queries, (((0,), (0,)), ((), ())), preferred_element_type=F32
        )

    def gather(chunk, weights, factor):
        piece, at = place(chunk)
        total[...] = total[...] * factor + jnp.dot(
            values[piece, at], weights[...], preferred_element_type=F32
        )

    def soften(chunk, scores, weights, top, mass, masked):
        s = scores[...]
        if masked:
            row = chunk * ROWS + lax.broadcasted_iota(jnp.int32, s.shape, 0)
            s = jnp.where((row >= start_ref[0]) & (row < end_ref[0]), s, NEGATIVE)
        new_top = jnp.maximum(top, jnp.max(s, axis=0, keepdims=True))
        exponents = jnp.exp2((s - new_top) * EXP2_SCALE)
        factor = jnp.exp2((top - new_top) * EXP2_SCALE)
        weights[...] = exponents.astype(BF16)
        return new_top, mass * factor + jnp.sum(exponents, axis=0, keepdims=True), factor

    total[...] = jnp.zeros_like(total)
    p1[...] = jnp.zeros_like(p1)
    low_pair, high_pair = low // 2, (high + 1) // 2
    score(2 * low_pair, s0)

    def step(pair, carried, masked):
        top, mass, factor = carried
        chunk = 2 * pair
        score(chunk + 1, s1)
        gather(jnp.maximum(chunk - 1, 0), p1, factor)
        top, mass, factor = soften(chunk, s0, p0, top, mass, masked)
        score(jnp.minimum(chunk + 2, CHUNKS - 1), s0)
        gather(chunk, p0, factor)
        return soften(chunk + 1, s1, p1, top, mass, masked)

    def one_pair(pair, carried):
        full = (start_last <= 2 * pair * ROWS) & (end_first >= (2 * pair + 2) * ROWS)
        return lax.cond(
            full, lambda c: step(pair, c, False), lambda c: step(pair, c, True), carried
        )

    first = (
        jnp.full((1, ROWS), NEGATIVE, F32),
        jnp.zeros((1, ROWS), F32),
        jnp.ones((1, ROWS), F32),
    )
    top, mass, factor = lax.fori_loop(low_pair, high_pair, one_pair, first)
    gather(2 * high_pair - 1, p1, factor)
    attended = jnp.transpose(total[...] / mass).astype(BF16)
    for y in range(NY):
        out_ref[y, 0, :, :HD] = attended[y * 96 : (y + 1) * 96]
    max_ref[0] = top


def attention(table, queries, starts, ends, pieces):
    whole = pl.BlockSpec(memory_space=pltpu.HBM)
    row = pl.BlockSpec((1, 1, ROWS), lambda i, t: (i, 0, 0))
    return pl.pallas_call(
        attention_kernel,
        out_shape=(
            jax.ShapeDtypeStruct((NY, NX, ROWS // NY, 128), BF16),
            jax.ShapeDtypeStruct((NX, 1, ROWS), F32),
        ),
        grid_spec=pltpu.PrefetchScalarGridSpec(
            num_scalar_prefetch=1,
            grid=(NX,),
            in_specs=[pl.BlockSpec((1, HD, ROWS), lambda i, t: (i, 0, 0)), row, row] + [whole] * 10,
            out_specs=(
                pl.BlockSpec((NY, 1, ROWS // NY, 128), lambda i, t: (0, i, 0, 0)),
                row,
            ),
            scratch_shapes=[
                pltpu.VMEM((8, NX, HD, ROWS), BF16),
                pltpu.VMEM((8, NX, HD, ROWS), BF16),
                pltpu.VMEM((ROWS, ROWS), F32),
                pltpu.VMEM((ROWS, ROWS), F32),
                pltpu.VMEM((ROWS, ROWS), BF16),
                pltpu.VMEM((ROWS, ROWS), BF16),
                pltpu.VMEM((HD, ROWS), F32),
                pltpu.SemaphoreType.DMA((20,)),
            ],
        ),
        compiler_params=params(14),
        name="attention",
    )(table, queries, starts, ends, *pieces)


def project_kernel(y_ref, att_ref, w0, w1, w2, w3, hidden_ref, bias_ref, gain_ref, shift_ref,
                   mixed_ref, normed_ref):
    y = y_ref[0]
    mixed = hidden_ref[...].astype(F32) + bias_ref[...]
    for k, w_ref in enumerate((w0, w1, w2, w3)):
        base = ((y - k) & 3) * 4
        for i in range(4):
            mixed = mixed + jnp.dot(att_ref[base + i, :, :HD], w_ref[i], preferred_element_type=F32)
    mixed_ref[...] = mixed
    mean = jnp.mean(mixed, axis=-1, keepdims=True)
    centered = mixed - mean
    var = jnp.mean(centered * centered, axis=-1, keepdims=True)
    normed = centered * lax.rsqrt(var + EPSILON) * gain_ref[...] + shift_ref[...]
    normed_ref[...] = normed.astype(BF16)


def project(y, attended, weights, hidden, bias, gain, shift):
    rows, width = ROWS // NY, hidden.shape[1]
    full = lambda *shape: pl.BlockSpec(shape, lambda i, t: (0,) * len(shape))
    return pl.pallas_call(
        project_kernel,
        out_shape=(
            jax.ShapeDtypeStruct((rows, width), F32),
            jax.ShapeDtypeStruct((rows, width), BF16),
        ),
        grid_spec=pltpu.PrefetchScalarGridSpec(
            num_scalar_prefetch=1,
            grid=(1,),
            in_specs=[full(16, rows, 128)]
            + [full(4, HD, width)] * 4
            + [pl.BlockSpec((rows, width), lambda i, t: (t[0], 0))]
            + [full(1, width)] * 3,
            out_specs=(full(rows, width), full(rows, width)),
        ),
        compiler_params=params(16),
        name="project",
    )(y, attended, *weights, hidden, bias, gain, shift)


def mlp_kernel(x0, x1, x2, x3, up_ref, bias_ref, down_ref, o0, o1, o2, o3, rows, total):
    step = pl.program_id(0)
    size = ROWS // NY

    @pl.when(step == 0)
    def _():
        for k, x in enumerate((x0, x1, x2, x3)):
            rows[k * size : (k + 1) * size] = x[...]

    units = jnp.dot(rows[...], up_ref[...], preferred_element_type=F32) + bias_ref[...]
    units = 0.5 * units * (1.0 + lax.erf(units * float(np.sqrt(0.5))))
    part = jnp.dot(units.astype(BF16), down_ref[...], preferred_element_type=F32)

    @pl.when(step == 0)
    def _():
        total[...] = part

    @pl.when(step > 0)
    def _():
        total[...] += part

    @pl.when(step == pl.num_programs(0) - 1)
    def _():
        for k, o in enumerate((o0, o1, o2, o3)):
            o[...] = total[k * size : (k + 1) * size].astype(o.dtype)


def mlp(pieces, up_weight, up_bias, down_weight):
    size, width = ROWS // NY, up_weight.shape[0]
    hidden = up_weight.shape[1]
    block = 384
    piece = pl.BlockSpec((size, width), lambda i: (0, 0))
    return pl.pallas_call(
        mlp_kernel,
        out_shape=[jax.ShapeDtypeStruct((size, width), F32 if k == 0 else BF16) for k in range(NY)],
        grid=(hidden // block,),
        in_specs=[piece] * 4
        + [
            pl.BlockSpec((width, block), lambda i: (0, i)),
            pl.BlockSpec((1, block), lambda i: (0, i)),
            pl.BlockSpec((block, width), lambda i: (i, 0)),
        ],
        out_specs=[piece] * 4,
        scratch_shapes=[pltpu.VMEM((ROWS, width), BF16), pltpu.VMEM((ROWS, width), F32)],
        compiler_params=params(16),
        name="mlp",
    )(*pieces, up_weight, up_bias, down_weight)


def merge_kernel(y_ref, x0, x1, x2, x3, weight_ref, bias_ref, out_ref, rows, total):
    step = pl.program_id(0)
    size = ROWS // NY
    groups = ROWS // 4

    @pl.when(step == 0)
    def _():
        for k, x in enumerate((x0, x1, x2, x3)):
            rows[k * size : (k + 1) * size] = x[...]

    at = lax.broadcasted_iota(jnp.int32, (groups, ROWS), 1)
    group = lax.broadcasted_iota(jnp.int32, (groups, ROWS), 0)
    piece = (at >= size).astype(jnp.int32) + (at >= 2 * size) + (at >= 3 * size)
    row = ((y_ref[0] - piece) & 3) * size + at - piece * size
    pick = (row == 4 * group + step).astype(F32).astype(BF16)
    chosen = jnp.dot(pick, rows[...], preferred_element_type=F32).astype(BF16)
    part = jnp.dot(chosen, weight_ref[...], preferred_element_type=F32)

    @pl.when(step == 0)
    def _():
        total[...] = part

    @pl.when(step > 0)
    def _():
        total[...] += part

    @pl.when(step == pl.num_programs(0) - 1)
    def _():
        out_ref[...] = (total[...] + bias_ref[...]).astype(BF16)


def merge(y, pieces, weight, bias):
    size, width = pieces[0].shape
    features = weight.shape[1]
    groups = ROWS // 4
    piece = pl.BlockSpec((size, width), lambda i, t: (0, 0))
    return pl.pallas_call(
        merge_kernel,
        out_shape=jax.ShapeDtypeStruct((groups, features), BF16),
        grid_spec=pltpu.PrefetchScalarGridSpec(
            num_scalar_prefetch=1,
            grid=(4,),
            in_specs=[piece] * 4
            + [
                pl.BlockSpec((width, features), lambda i, t: (i, 0)),
                pl.BlockSpec((1, features), lambda i, t: (0, 0)),
            ],
            out_specs=pl.BlockSpec((groups, features), lambda i, t: (0, 0)),
            scratch_shapes=[pltpu.VMEM((ROWS, width), BF16), pltpu.VMEM((groups, features), F32)],
        ),
        compiler_params=params(16),
        name="merge",
    )(y, *pieces, weight, bias)


def body(
    hidden_in,
    queries,
    keys,
    values,
    out_weight,
    out_bias,
    norm_gain,
    norm_bias,
    up_weight,
    up_bias,
    down_weight,
    down_bias,
    merge_weight,
    merge_bias,
    group_segments,
    owner_slots,
):
    heads = 4
    width = hidden_in.shape[1]
    request_total = owner_slots.shape[0]
    x = lax.axis_index("x")
    y = lax.axis_index("y")
    z = lax.axis_index("z")
    c = lax.axis_index("c")
    y_scalar = jnp.reshape(y, (1,)).astype(jnp.int32)

    swap = [(0, 1), (1, 0)]
    key_parts = keys.T.reshape(heads, HD, ROWS)
    value_parts = values.T.reshape(heads, HD, ROWS)
    query_parts = queries.T.reshape(heads, HD, ROWS)
    both_parts = jnp.concatenate([key_parts, value_parts], axis=1)
    own = lax.all_to_all(both_parts, "x", 0, 0)
    behind = lax.ppermute(own, "z", ring(NZ, 1))
    ahead = lax.ppermute(own, "z", ring(NZ, NZ - 1))
    own_c = lax.ppermute(own, "c", swap)
    spread = jnp.broadcast_to(group_segments, (CHUNKS,) + group_segments.shape)
    spread, _ = lax.optimization_barrier((spread, own))
    all_segments = lax.all_to_all(spread, ("x", "z", "c"), 0, 0, tiled=True)
    query_parts, _ = lax.optimization_barrier((query_parts, all_segments))
    query_own = lax.all_to_all(query_parts, "x", 0, 0)
    behind_c = lax.ppermute(behind, "c", swap)
    ahead_c = lax.ppermute(ahead, "c", swap)
    far_a = lax.ppermute(behind[:2], "z", ring(NZ, 1))
    far_b = lax.ppermute(ahead[2:], "z", ring(NZ, NZ - 1))
    far_a_in, far_b_in, query_own = lax.optimization_barrier((far_a, far_b, query_own))
    far_a_c = lax.ppermute(far_a_in, "c", swap)
    far_b_c = lax.ppermute(far_b_in, "c", swap)
    pieces = [own, behind, ahead, far_a, far_b, own_c, behind_c, ahead_c, far_a_c, far_b_c]
    pieces = [in_hbm(piece) for piece in pieces]

    requests = jnp.arange(request_total, dtype=jnp.int32)
    group_rows = jnp.take(
        all_segments.reshape(NX, NZ * NC, ROWS // 4), z * NC + c, axis=1
    )
    counts = 4.0 * jnp.sum(
        (all_segments.reshape(1, -1) == requests[:, None]).astype(F32), axis=1
    )
    row_segments = jnp.repeat(group_rows, 4, axis=1)
    below = requests[:, None, None] < row_segments[None]
    upto = requests[:, None, None] <= row_segments[None]
    starts = jnp.sum(jnp.where(below, counts[:, None, None], 0.0), axis=0).astype(jnp.int32)
    ends = jnp.sum(jnp.where(upto, counts[:, None, None], 0.0), axis=0).astype(jnp.int32)
    table = jnp.stack(
        [
            starts[:, 0] // ROWS,
            (ends[:, -1] + ROWS - 1) // ROWS,
            starts[:, -1],
            ends[:, 0],
            jnp.stack([z, c, z, c]).astype(jnp.int32),
        ]
    )
    attended, row_max = attention(
        table, query_own, starts[:, None], ends[:, None], pieces
    )

    attended = lax.all_to_all(attended.reshape(16, ROWS // NY, 128), ("y", "x"), 0, 0)
    weights = [
        w.reshape(heads, HD, width) for w in [out_weight] + shifted(out_weight, "y", NY)
    ]
    mixed, normed = project(
        y_scalar, attended, weights, hidden_in, out_bias[None], norm_gain[None], norm_bias[None]
    )

    normed_all = [normed] + shifted(normed, "y", NY)
    down = mlp(normed_all, in_hbm(up_weight), up_bias[None], in_hbm(down_weight))
    state = mixed + down_bias + down[0]
    for k in range(1, NY):
        back = lax.ppermute(down[k], "y", ring(NY, NY - k))
        state = state + back.astype(F32)
    state_bf = state.astype(BF16)
    merged_out = merge(
        y_scalar, [state_bf] + shifted(state_bf, "y", NY), in_hbm(merge_weight), merge_bias[None]
    )

    member = row_segments[None] == requests[:, None, None]
    request_max = jnp.max(jnp.where(member, row_max[:, 0][None], NEGATIVE), axis=(1, 2))
    request_max = request_max * (HD**-0.5)
    squares = jnp.sum(state * state, axis=-1)
    own_groups = lax.dynamic_slice_in_dim(group_segments, y * (ROWS // 16), ROWS // 16)
    own_rows = jnp.repeat(own_groups, 4)
    sums = jnp.sum(jnp.where(own_rows[None] == requests[:, None], squares[None], 0.0), axis=1)
    chosen = owner_slots[None, :] == jnp.arange(request_total, dtype=jnp.int32)[:, None]
    slot_sums = jnp.sum(jnp.where(chosen, sums[None], 0.0), axis=1)
    slot_max = jnp.sum(jnp.where(chosen, request_max[None], 0.0), axis=1)
    slot_counts = jnp.sum(jnp.where(chosen, counts[None], 0.0), axis=1)
    sent = jnp.concatenate([slot_sums.reshape(CHUNKS, 2), slot_max.reshape(CHUNKS, 2)], axis=1)
    sent = jnp.pad(sent, ((0, 0), (0, 124)))
    sent = jnp.broadcast_to(sent[None], (NY,) + sent.shape).reshape(NY * CHUNKS, 128)
    got = lax.all_to_all(sent, ("y", "x", "z", "c"), 0, 0, tiled=True)
    got = got.reshape(NY, NX, NZ * NC, 128)
    here = (x * (NZ * NC) + z * NC + c) * 2
    own_sums = jnp.sum(got[..., :2], axis=(0, 1, 2))
    own_counts = lax.dynamic_slice_in_dim(slot_counts, here, 2)
    state_rms = jnp.sqrt(own_sums / (own_counts * width) + EPSILON)
    plane = lax.dynamic_index_in_dim(got[..., 2:4], y, 0, keepdims=False)
    logit_max = jnp.transpose(jnp.max(plane, axis=1))
    return (merged_out, state_rms, logit_max)


def solution(mesh):
    fine = Mesh(mesh.devices.reshape(NY, NX, NZ, NC), ("y", "x", "z", "c"))
    blk = ("x", "z", "c")
    in_specs = (
        P(blk, None),
        P(blk, "y"),
        P(blk, "y"),
        P(blk, "y"),
        P("y", None),
        P(),
        P(),
        P(),
        P(None, "y"),
        P("y"),
        P("y", None),
        P(),
        P(None, "y"),
        P("y"),
        P(blk),
        P(),
    )
    out_specs = (P(blk, "y"), P(blk), P(blk, "y"))
    return jax.shard_map(body, mesh=fine, in_specs=in_specs, out_specs=out_specs, check_vma=False)
```

```python
import functools

import jax
import jax.numpy as jnp
import numpy as np
from jax import lax
from jax.experimental import pallas as pl
from jax.experimental.pallas import tpu as pltpu
from jax.sharding import Mesh
from jax.sharding import PartitionSpec as P

HD = 88
NEGATIVE = -1e30
EPSILON = 1e-06
F32 = jnp.float32
BF16 = jnp.bfloat16

NY, NX, NZ, NC = 4, 4, 4, 2
ROWS = 384
CHUNKS = NX * NZ * NC
REQUESTS = 64
MARK_AT, QUERY_AT = 2 * HD, 2 * HD + 8
EXP2_SCALE = float(np.log2(np.e) / np.sqrt(HD))


def ring(size, shift):
    return [(i, (i + shift) % size) for i in range(size)]


def shifted(value, axis, size):
    order = [1, size - 1] + list(range(2, size - 1)) if size > 2 else [1]
    got = {k: lax.ppermute(value, axis, ring(size, k)) for k in order}
    return [got[k] for k in range(1, size)]


def in_hbm(value):
    return pltpu.with_memory_space_constraint(value, pltpu.HBM)


def params(mib):
    return pltpu.CompilerParams(vmem_limit_bytes=mib << 20)


def attention_kernel(first, last, layout, *refs):
    count = len(layout)
    own, pieces, refs = refs[0], refs[1 : 1 + count], refs[1 + count :]
    if not first:
        top_in, mass_in, total_in = refs[:3]
        refs = refs[3:]
    if last:
        out_ref, top_ref = refs[:2]
        refs = refs[2:]
    else:
        top_ref, mass_ref, total_ref = refs[:3]
        refs = refs[3:]
    if last:
        mass_ref, total_ref = refs[:2]
        refs = refs[2:]
        mass, total = mass_ref, total_ref
        mass_at, total_at = mass_ref, total_ref
    else:
        mass_at, total_at = mass_ref.at[0], total_ref.at[0]
    top_at = top_ref.at[0]
    queries, marks, keys, values, key_marks, spread, s0, s1, p0, p1, ends, sems = refs
    part = pl.program_id(0)

    @pl.when(part == 0)
    def _():
        copies = [(own.at[:, pl.ds(QUERY_AT, HD)], queries), (own.at[:, pl.ds(MARK_AT, 8)], marks)]
        for piece, (slot, at, size) in zip(pieces, layout):
            at = pl.ds(at, size)
            copies.append((piece.at[:, pl.ds(0, HD)], keys.at[slot, at]))
            copies.append((piece.at[:, pl.ds(HD, HD)], values.at[slot, at]))
            copies.append((piece.at[:, pl.ds(MARK_AT, 8)], key_marks.at[slot, at]))
        copies = [pltpu.make_async_copy(*c, sems.at[i]) for i, c in enumerate(copies)]
        for copy in copies:
            copy.start()
        for copy in copies:
            copy.wait()
        for slot in range(2):
            for x in range(NX):
                mark = key_marks[slot, x][:1].astype(F32)
                ends[slot, x, 0] = jnp.min(mark)
                ends[slot, x, 1] = jnp.max(mark)

    mark = marks[part][:1].astype(F32)
    q_first, q_last = jnp.min(mark), jnp.max(mark)
    requests = lax.broadcasted_iota(jnp.int32, (REQUESTS, ROWS), 0).astype(F32)
    spread[...] = jnp.where(requests == mark, 1.0, 0.0).astype(BF16)
    low, high = jnp.int32(NX), jnp.int32(0)
    for x in range(NX):
        active = (ends[0, x, 1] >= q_first) & (ends[0, x, 0] <= q_last)
        active = active | ((ends[1, x, 1] >= q_first) & (ends[1, x, 0] <= q_last))
        low = jnp.where(active & (low == NX), x, low)
        high = jnp.where(active, x + 1, high)

    if first:
        top_at[...] = jnp.full((1, ROWS), NEGATIVE, F32)
        mass_at[...] = jnp.zeros((1, ROWS), F32)
        total_at[...] = jnp.zeros((HD, ROWS), F32)
    else:
        top_at[...] = top_in[0]
        mass_at[...] = mass_in[0]
        total_at[...] = total_in[0]

    def both(a, b):
        return lax.dot_general(a, b, (((0,), (0,)), ((), ())), preferred_element_type=F32)

    def score(slot, x, scores):
        scores[...] = both(keys[slot, x], queries[part])

    def gather(slot, x, weights, factor):
        total_at[...] = total_at[...] * factor + jnp.dot(
            values[slot, x], weights[...], preferred_element_type=F32
        )

    def soften(slot, x, scores, weights, top, mass, masked):
        s = scores[...]
        if masked:
            key_mark = key_marks[slot, x][:1].astype(F32)
            key_spread = jnp.where(requests == key_mark, 1.0, 0.0).astype(BF16)
            s = jnp.where(both(key_spread, spread[...]) > 0.5, s, NEGATIVE)
        new_top = jnp.maximum(top, jnp.max(s, axis=0, keepdims=True))
        exponents = jnp.exp2((s - new_top) * EXP2_SCALE)
        factor = jnp.exp2((top - new_top) * EXP2_SCALE)
        weights[...] = exponents.astype(BF16)
        return new_top, mass * factor + jnp.sum(exponents, axis=0, keepdims=True), factor

    def step(x, carried, masked):
        top, mass, factor = carried
        score(1, x, s1)
        gather(1, jnp.maximum(x - 1, 0), p1, factor)
        top, mass, factor = soften(0, x, s0, p0, top, mass, masked)
        score(0, jnp.minimum(x + 1, NX - 1), s0)
        gather(0, x, p0, factor)
        return soften(1, x, s1, p1, top, mass, masked)

    def one_pair(x, carried):
        full = q_first == q_last
        for slot in range(2):
            full = full & (ends[slot, x, 0] == q_first) & (ends[slot, x, 1] == q_first)
        return lax.cond(full, lambda c: step(x, c, False), lambda c: step(x, c, True), carried)

    @pl.when(high > low)
    def _():
        p1[...] = jnp.zeros_like(p1)
        score(0, low, s0)
        start = (top_at[...], mass_at[...], jnp.ones((1, ROWS), F32))
        top, mass, factor = lax.fori_loop(low, high, one_pair, start)
        gather(1, high - 1, p1, factor)
        top_at[...] = top
        mass_at[...] = mass

    if last:
        attended = jnp.transpose(total_at[...] / mass_at[...]).astype(BF16)
        for y in range(NY):
            out_ref[y, 0, :, :HD] = attended[y * 96 : (y + 1) * 96]


def attention_pass(own, pieces, layout, state, last):
    whole = pl.BlockSpec(memory_space=pltpu.HBM)
    row = pl.BlockSpec((1, 1, ROWS), lambda i: (i, 0, 0))
    block = pl.BlockSpec((1, HD, ROWS), lambda i: (i, 0, 0))
    rows = jax.ShapeDtypeStruct((NX, 1, ROWS), F32)
    scratch = [
        pltpu.VMEM((NX, HD, ROWS), BF16),
        pltpu.VMEM((NX, 8, ROWS), BF16),
        pltpu.VMEM((2, NX, HD, ROWS), BF16),
        pltpu.VMEM((2, NX, HD, ROWS), BF16),
        pltpu.VMEM((2, NX, 8, ROWS), BF16),
        pltpu.VMEM((REQUESTS, ROWS), BF16),
        pltpu.VMEM((ROWS, ROWS), F32),
        pltpu.VMEM((ROWS, ROWS), F32),
        pltpu.VMEM((ROWS, ROWS), BF16),
        pltpu.VMEM((ROWS, ROWS), BF16),
        pltpu.SMEM((2, NX, 2), F32),
        pltpu.SemaphoreType.DMA((2 + 3 * len(layout),)),
    ]
    if last:
        out_shape = (jax.ShapeDtypeStruct((NY, NX, ROWS // NY, 128), BF16), rows)
        out_specs = (pl.BlockSpec((NY, 1, ROWS // NY, 128), lambda i: (0, i, 0, 0)), row)
        scratch = [pltpu.VMEM((1, ROWS), F32), pltpu.VMEM((HD, ROWS), F32)] + scratch
    else:
        out_shape = (rows, rows, jax.ShapeDtypeStruct((NX, HD, ROWS), F32))
        out_specs = (row, row, block)
    pairs = NX * NX * 2 * ROWS * ROWS
    return pl.pallas_call(
        functools.partial(attention_kernel, not state, last, layout),
        out_shape=out_shape,
        grid=(NX,),
        in_specs=[whole] * (1 + len(pieces)) + [row, row, block][: len(state)],
        out_specs=out_specs,
        scratch_shapes=scratch,
        compiler_params=params(12),
        cost_estimate=pl.CostEstimate(
            flops=12 * pairs * HD, transcendentals=pairs, bytes_accessed=4 << 20
        ),
        name="attention_last" if last else "attention_pass",
    )(in_hbm(own), *[in_hbm(piece) for piece in pieces], *state)


def project_kernel(y_ref, att_ref, w0, w1, w2, w3, hidden_ref, bias_ref, gain_ref, shift_ref,
                   mixed_ref, normed_ref):
    y = y_ref[0]
    mixed = hidden_ref[...].astype(F32) + bias_ref[...]
    for k, w_ref in enumerate((w0, w1, w2, w3)):
        base = ((y - k) & 3) * 4
        for i in range(4):
            mixed = mixed + jnp.dot(att_ref[base + i, :, :HD], w_ref[i], preferred_element_type=F32)
    mixed_ref[...] = mixed
    mean = jnp.mean(mixed, axis=-1, keepdims=True)
    centered = mixed - mean
    var = jnp.mean(centered * centered, axis=-1, keepdims=True)
    normed = centered * lax.rsqrt(var + EPSILON) * gain_ref[...] + shift_ref[...]
    normed_ref[...] = normed.astype(BF16)


def project(y, attended, weights, hidden, bias, gain, shift):
    rows, width = ROWS // NY, hidden.shape[1]
    full = lambda *shape: pl.BlockSpec(shape, lambda i, t: (0,) * len(shape))
    return pl.pallas_call(
        project_kernel,
        out_shape=(
            jax.ShapeDtypeStruct((rows, width), F32),
            jax.ShapeDtypeStruct((rows, width), BF16),
        ),
        grid_spec=pltpu.PrefetchScalarGridSpec(
            num_scalar_prefetch=1,
            grid=(1,),
            in_specs=[full(16, rows, 128)]
            + [full(4, HD, width)] * 4
            + [pl.BlockSpec((rows, width), lambda i, t: (t[0], 0))]
            + [full(1, width)] * 3,
            out_specs=(full(rows, width), full(rows, width)),
        ),
        compiler_params=params(16),
        name="project",
    )(y, attended, *weights, hidden, bias, gain, shift)


def mlp_kernel(x_ref, up_ref, bias_ref, down_ref, out_ref, total):
    step = pl.program_id(0)
    units = jnp.dot(x_ref[...], up_ref[...], preferred_element_type=F32) + bias_ref[...]
    units = 0.5 * units * (1.0 + lax.erf(units * float(np.sqrt(0.5))))
    part = jnp.dot(units.astype(BF16), down_ref[...], preferred_element_type=F32)

    @pl.when(step == 0)
    def _():
        total[...] = part

    @pl.when(step > 0)
    def _():
        total[...] += part

    @pl.when(step == pl.num_programs(0) - 1)
    def _():
        out_ref[...] = total[...].astype(out_ref.dtype)


def mlp(rows, up_weight, up_bias, down_weight, dtype):
    size, width = rows.shape
    hidden = up_weight.shape[1]
    block = 512
    whole = pl.BlockSpec((size, width), lambda i: (0, 0))
    return pl.pallas_call(
        mlp_kernel,
        out_shape=jax.ShapeDtypeStruct((size, width), dtype),
        grid=(hidden // block,),
        in_specs=[
            whole,
            pl.BlockSpec((width, block), lambda i: (0, i)),
            pl.BlockSpec((1, block), lambda i: (0, i)),
            pl.BlockSpec((block, width), lambda i: (i, 0)),
        ],
        out_specs=whole,
        scratch_shapes=[pltpu.VMEM((size, width), F32)],
        compiler_params=params(12),
        cost_estimate=pl.CostEstimate(
            flops=4 * size * width * hidden,
            transcendentals=size * hidden,
            bytes_accessed=4 * width * hidden,
        ),
        name="mlp",
    )(rows, up_weight, up_bias, down_weight)


def merge_kernel(y_ref, x0, x1, x2, x3, weight_ref, bias_ref, out_ref, rows, total):
    step = pl.program_id(0)
    size = ROWS // NY
    groups = ROWS // 4

    @pl.when(step == 0)
    def _():
        for k, x in enumerate((x0, x1, x2, x3)):
            rows[k * size : (k + 1) * size] = x[...]

    at = lax.broadcasted_iota(jnp.int32, (groups, ROWS), 1)
    group = lax.broadcasted_iota(jnp.int32, (groups, ROWS), 0)
    piece = (at >= size).astype(jnp.int32) + (at >= 2 * size) + (at >= 3 * size)
    row = ((y_ref[0] - piece) & 3) * size + at - piece * size
    pick = (row == 4 * group + step).astype(F32).astype(BF16)
    chosen = jnp.dot(pick, rows[...], preferred_element_type=F32).astype(BF16)
    part = jnp.dot(chosen, weight_ref[...], preferred_element_type=F32)

    @pl.when(step == 0)
    def _():
        total[...] = part

    @pl.when(step > 0)
    def _():
        total[...] += part

    @pl.when(step == pl.num_programs(0) - 1)
    def _():
        out_ref[...] = (total[...] + bias_ref[...]).astype(BF16)


def merge(y, pieces, weight, bias):
    size, width = pieces[0].shape
    features = weight.shape[1]
    groups = ROWS // 4
    piece = pl.BlockSpec((size, width), lambda i, t: (0, 0))
    return pl.pallas_call(
        merge_kernel,
        out_shape=jax.ShapeDtypeStruct((groups, features), BF16),
        grid_spec=pltpu.PrefetchScalarGridSpec(
            num_scalar_prefetch=1,
            grid=(4,),
            in_specs=[piece] * 4
            + [
                pl.BlockSpec((width, features), lambda i, t: (i, 0)),
                pl.BlockSpec((1, features), lambda i, t: (0, 0)),
            ],
            out_specs=pl.BlockSpec((groups, features), lambda i, t: (0, 0)),
            scratch_shapes=[pltpu.VMEM((ROWS, width), BF16), pltpu.VMEM((groups, features), F32)],
        ),
        compiler_params=params(16),
        name="merge",
    )(y, *pieces, weight, bias)


def body(
    hidden_in,
    queries,
    keys,
    values,
    out_weight,
    out_bias,
    norm_gain,
    norm_bias,
    up_weight,
    up_bias,
    down_weight,
    down_bias,
    merge_weight,
    merge_bias,
    group_segments,
    owner_slots,
):
    heads = 4
    width = hidden_in.shape[1]
    request_total = owner_slots.shape[0]
    y = lax.axis_index("y")
    y_scalar = jnp.reshape(y, (1,)).astype(jnp.int32)

    swap = [(0, 1), (1, 0)]
    requests = jnp.arange(request_total, dtype=jnp.int32)
    key_parts = keys.T.reshape(heads, HD, ROWS)
    value_parts = values.T.reshape(heads, HD, ROWS)
    query_parts = queries.T.reshape(heads, HD, ROWS)
    marks = jnp.broadcast_to(jnp.repeat(group_segments, 4).astype(BF16), (heads, 8, ROWS))
    parts = jnp.concatenate([key_parts, value_parts, marks, query_parts], axis=1)
    own = lax.all_to_all(parts, "x", 0, 0)
    sent = own[:, :QUERY_AT]
    behind = lax.ppermute(sent, "z", ring(NZ, 1))
    ahead = lax.ppermute(sent, "z", ring(NZ, NZ - 1))
    own_c = lax.ppermute(sent, "c", swap)
    pair = ((0, 0, 4), (1, 0, 4))
    state = attention_pass(own, [own, own_c], pair, (), False)
    behind, ahead, state = lax.optimization_barrier((behind, ahead, state))
    behind_c = lax.ppermute(behind, "c", swap)
    ahead_c = lax.ppermute(ahead, "c", swap)
    far_a = lax.ppermute(behind[:2], "z", ring(NZ, 1))
    far_b = lax.ppermute(ahead[2:], "z", ring(NZ, NZ - 1))
    state = attention_pass(own, [behind, ahead], pair, state, False)
    far_a, far_b, state = lax.optimization_barrier((far_a, far_b, state))
    far_a_c = lax.ppermute(far_a, "c", swap)
    far_b_c = lax.ppermute(far_b, "c", swap)
    state = attention_pass(own, [behind_c, ahead_c], pair, state, False)
    attended, row_max = attention_pass(
        own,
        [far_a, far_b, far_a_c, far_b_c],
        ((0, 0, 2), (0, 2, 2), (1, 0, 2), (1, 2, 2)),
        state,
        True,
    )
    row_segments = own[:, MARK_AT].astype(jnp.int32)

    attended = lax.all_to_all(attended.reshape(16, ROWS // NY, 128), ("y", "x"), 0, 0)
    weights = [
        w.reshape(heads, HD, width) for w in [out_weight] + shifted(out_weight, "y", NY)
    ]
    mixed, normed = project(
        y_scalar, attended, weights, hidden_in, out_bias[None], norm_gain[None], norm_bias[None]
    )

    normed_all = [normed] + shifted(normed, "y", NY)
    layer = (in_hbm(up_weight), up_bias[None], in_hbm(down_weight))
    back = [None] * NY
    part = normed
    for k in (0, 1, 3, 2):
        rows, _ = lax.optimization_barrier((normed_all[k], part))
        part = mlp(rows, *layer, F32 if k == 0 else BF16)
        back[k] = part if k == 0 else lax.ppermute(part, "y", ring(NY, NY - k))
    state = mixed + down_bias + back[0]
    for k in range(1, NY):
        state = state + back[k].astype(F32)
    state_bf = state.astype(BF16)
    merged_out = merge(
        y_scalar, [state_bf] + shifted(state_bf, "y", NY), in_hbm(merge_weight), merge_bias[None]
    )

    member = row_segments[None] == requests[:, None, None]
    request_max = jnp.max(jnp.where(member, row_max[:, 0][None], NEGATIVE), axis=(1, 2))
    request_max = request_max * (HD**-0.5)
    squares = jnp.sum(state * state, axis=-1)
    own_groups = lax.dynamic_slice_in_dim(group_segments, y * (ROWS // 16), ROWS // 16)
    own_rows = jnp.repeat(own_groups, 4)
    sums = jnp.sum(jnp.where(own_rows[None] == requests[:, None], squares[None], 0.0), axis=1)
    chosen = owner_slots[None, :] == jnp.arange(request_total, dtype=jnp.int32)[:, None]
    slot_sums = jnp.sum(jnp.where(chosen, sums[None], 0.0), axis=1)
    slot_max = jnp.sum(jnp.where(chosen, request_max[None], 0.0), axis=1)
    own_counts = jnp.sum((own_rows[None] == requests[:, None]).astype(F32), axis=1)
    slot_counts = jnp.sum(jnp.where(chosen, own_counts[None], 0.0), axis=1)
    sent = [slot_sums, slot_max, slot_counts]
    sent = jnp.concatenate([value.reshape(CHUNKS, 2) for value in sent], axis=1)
    sent = jnp.pad(sent, ((0, 0), (0, 122)))
    sent = jnp.broadcast_to(sent[None], (NY,) + sent.shape).reshape(NY * CHUNKS, 128)
    got = lax.all_to_all(sent, ("y", "x", "z", "c"), 0, 0, tiled=True)
    got = got.reshape(NY, NX, NZ * NC, 128)
    own_sums = jnp.sum(got[..., :2], axis=(0, 1, 2))
    own_counts = jnp.sum(got[..., 4:6], axis=(0, 1, 2))
    state_rms = jnp.sqrt(own_sums / (own_counts * width) + EPSILON)
    plane = lax.dynamic_index_in_dim(got[..., 2:4], y, 0, keepdims=False)
    logit_max = jnp.transpose(jnp.max(plane, axis=1))
    return (merged_out, state_rms, logit_max)


def solution(mesh):
    fine = Mesh(mesh.devices.reshape(NY, NX, NZ, NC), ("y", "x", "z", "c"))
    blk = ("x", "z", "c")
    in_specs = (
        P(blk, None),
        P(blk, "y"),
        P(blk, "y"),
        P(blk, "y"),
        P("y", None),
        P(),
        P(),
        P(),
        P(None, "y"),
        P("y"),
        P("y", None),
        P(),
        P(None, "y"),
        P("y"),
        P(blk),
        P(),
    )
    out_specs = (P(blk, "y"), P(blk), P(blk, "y"))
    return jax.shard_map(body, mesh=fine, in_specs=in_specs, out_specs=out_specs, check_vma=False)
```

```python
import functools

import jax
import jax.numpy as jnp
import numpy as np
from jax import lax
from jax.experimental import pallas as pl
from jax.experimental.pallas import tpu as pltpu
from jax.sharding import Mesh
from jax.sharding import PartitionSpec as P

HD = 88
NEGATIVE = -1e30
EPSILON = 1e-06
F32 = jnp.float32
BF16 = jnp.bfloat16

NY, NX, NZ, NC = 4, 4, 4, 2
ROWS = 384
CHUNKS = NX * NZ * NC
REQUESTS = 64
MARK_AT, QUERY_AT = 2 * HD, 2 * HD + 8
EXP2_SCALE = float(np.log2(np.e) / np.sqrt(HD))


def ring(size, shift):
    return [(i, (i + shift) % size) for i in range(size)]


def shifted(value):
    near = [lax.ppermute(value, "y", ring(NY, k)) for k in (1, 3)]
    half = value.shape[0] // 2
    far = [lax.ppermute(part, "y", ring(NY, 2)) for part in (value[:half], value[half:])]
    return near[0], far[0], far[1], near[1]


def in_hbm(value):
    return pltpu.with_memory_space_constraint(value, pltpu.HBM)


def params(mib):
    return pltpu.CompilerParams(vmem_limit_bytes=mib << 20)


def attention_kernel(first, last, per_x, layout, place_ref, *refs):
    count = len(layout)
    own, pieces, refs = refs[0], refs[1 : 1 + count], refs[1 + count :]
    if not first:
        top_in, mass_in, total_in = refs[:3]
        refs = refs[3:]
    if last:
        out_ref, top_ref, mass_at, total_at = refs[:4]
        refs = refs[4:]
    else:
        top_ref, mass_ref, total_ref = refs[:3]
        refs = refs[3:]
        mass_at, total_at = mass_ref.at[0], total_ref.at[0]
    top_at = top_ref.at[0]
    queries, marks, keys, values, key_marks, spread, s0, s1, p0, p1, ends, own_ends, sems = refs
    part = pl.program_id(0)
    x_here, z_here = place_ref[0], place_ref[1]
    steps = NX * per_x

    @pl.when(part == 0)
    def _():
        copies = [(own.at[:, pl.ds(QUERY_AT, HD)], queries), (own.at[:, pl.ds(MARK_AT, 8)], marks)]
        for piece, (slot, at, size) in zip(pieces, layout):
            at = pl.ds(at, size)
            copies.append((piece.at[:, pl.ds(0, HD)], keys.at[slot, at]))
            copies.append((piece.at[:, pl.ds(HD, HD)], values.at[slot, at]))
            copies.append((piece.at[:, pl.ds(MARK_AT, 8)], key_marks.at[slot, at]))
        copies = [pltpu.make_async_copy(*c, sems.at[i]) for i, c in enumerate(copies)]
        for copy in copies:
            copy.start()
        for copy in copies:
            copy.wait()
        for k in range(NX):
            mark = marks[k][:1].astype(F32)
            own_ends[k, 0] = jnp.min(mark)
            own_ends[k, 1] = jnp.max(mark)
            for pair in range(per_x):
                even = key_marks[2 * pair, k][:1].astype(F32)
                odd = key_marks[2 * pair + 1, k][:1].astype(F32)
                ends[pair, k, 0] = jnp.min(jnp.minimum(even, odd))
                ends[pair, k, 1] = jnp.max(jnp.maximum(even, odd))

    def locate(t):
        if per_x == 1:
            return 0, (x_here - t) & 3
        x_of = t // per_x
        z_of = t - x_of * per_x
        z_of = z_of + (z_of >= z_here).astype(jnp.int32)
        return ((z_here - z_of) & 3) - 1, (x_here - x_of) & 3

    here = (x_here - part) & 3
    mark = marks[here][:1].astype(F32)
    q_first, q_last = own_ends[here, 0], own_ends[here, 1]
    requests = lax.broadcasted_iota(jnp.int32, (REQUESTS, ROWS), 0).astype(F32)
    spread[...] = jnp.where(requests == mark, 1.0, 0.0).astype(BF16)
    low, high = jnp.int32(steps), jnp.int32(0)
    for t in range(steps):
        pair, at = locate(jnp.int32(t))
        active = (ends[pair, at, 1] >= q_first) & (ends[pair, at, 0] <= q_last)
        low = jnp.where(active & (low == steps), t, low)
        high = jnp.where(active, t + 1, high)

    if first:
        top_at[...] = jnp.full((1, ROWS), NEGATIVE, F32)
        mass_at[...] = jnp.zeros((1, ROWS), F32)
        total_at[...] = jnp.zeros((HD, ROWS), F32)
    else:
        top_at[...] = top_in[0]
        mass_at[...] = mass_in[0]
        total_at[...] = total_in[0]

    def both(a, b):
        return lax.dot_general(a, b, (((0,), (0,)), ((), ())), preferred_element_type=F32)

    def score(slot, at, scores):
        scores[...] = both(keys[slot, at], queries[here])

    def gather(slot, at, weights, factor):
        total_at[...] = total_at[...] * factor + jnp.dot(
            values[slot, at], weights[...], preferred_element_type=F32
        )

    def soften(slot, at, scores, weights, top, mass, masked):
        s = scores[...]
        if masked:
            key_mark = key_marks[slot, at][:1].astype(F32)
            key_spread = jnp.where(requests == key_mark, 1.0, 0.0).astype(BF16)
            s = jnp.where(both(key_spread, spread[...]) > 0.5, s, NEGATIVE)
        new_top = jnp.maximum(top, jnp.max(s, axis=0, keepdims=True))
        exponents = jnp.exp2((s - new_top) * EXP2_SCALE)
        factor = jnp.exp2((top - new_top) * EXP2_SCALE)
        weights[...] = exponents.astype(BF16)
        return new_top, mass * factor + jnp.sum(exponents, axis=0, keepdims=True), factor

    def step(t, pair, at, carried, masked):
        top, mass, factor = carried
        old_pair, old_at = locate(jnp.maximum(t - 1, 0))
        new_pair, new_at = locate(jnp.minimum(t + 1, steps - 1))
        score(2 * pair + 1, at, s1)
        gather(2 * old_pair + 1, old_at, p1, factor)
        top, mass, factor = soften(2 * pair, at, s0, p0, top, mass, masked)
        score(2 * new_pair, new_at, s0)
        gather(2 * pair, at, p0, factor)
        return soften(2 * pair + 1, at, s1, p1, top, mass, masked)

    def one_pair(t, carried):
        pair, at = locate(t)
        full = (q_first == q_last) & (ends[pair, at, 0] == q_first) & (ends[pair, at, 1] == q_first)
        return lax.cond(
            full,
            lambda c: step(t, pair, at, c, False),
            lambda c: step(t, pair, at, c, True),
            carried,
        )

    @pl.when(high > low)
    def _():
        p1[...] = jnp.zeros_like(p1)
        pair, at = locate(low)
        score(2 * pair, at, s0)
        start = (top_at[...], mass_at[...], jnp.ones((1, ROWS), F32))
        top, mass, factor = lax.fori_loop(low, high, one_pair, start)
        pair, at = locate(high - 1)
        gather(2 * pair + 1, at, p1, factor)
        top_at[...] = top
        mass_at[...] = mass

    if last:
        attended = jnp.transpose(total_at[...] / mass_at[...]).astype(BF16)
        for y in range(NY):
            out_ref[y, 0, :, :HD] = attended[y * 96 : (y + 1) * 96]


def attention_pass(place, own, pieces, layout, state, last):
    per_x = 3 if state else 1
    slots = 2 * per_x
    whole = pl.BlockSpec(memory_space=pltpu.HBM)
    row = pl.BlockSpec((1, 1, ROWS), lambda i, t: (i, 0, 0))
    block = pl.BlockSpec((1, HD, ROWS), lambda i, t: (i, 0, 0))
    rows = jax.ShapeDtypeStruct((NX, 1, ROWS), F32)
    scratch = [
        pltpu.VMEM((NX, HD, ROWS), BF16),
        pltpu.VMEM((NX, 8, ROWS), BF16),
        pltpu.VMEM((slots, NX, HD, ROWS), BF16),
        pltpu.VMEM((slots, NX, HD, ROWS), BF16),
        pltpu.VMEM((slots, NX, 8, ROWS), BF16),
        pltpu.VMEM((REQUESTS, ROWS), BF16),
        pltpu.VMEM((ROWS, ROWS), F32),
        pltpu.VMEM((ROWS, ROWS), F32),
        pltpu.VMEM((ROWS, ROWS), BF16),
        pltpu.VMEM((ROWS, ROWS), BF16),
        pltpu.SMEM((per_x, NX, 2), F32),
        pltpu.SMEM((NX, 2), F32),
        pltpu.SemaphoreType.DMA((2 + 3 * len(layout),)),
    ]
    if last:
        out_shape = (jax.ShapeDtypeStruct((NY, NX, ROWS // NY, 128), BF16), rows)
        out_specs = (pl.BlockSpec((NY, 1, ROWS // NY, 128), lambda i, t: (0, i, 0, 0)), row)
        scratch = [pltpu.VMEM((1, ROWS), F32), pltpu.VMEM((HD, ROWS), F32)] + scratch
    else:
        out_shape = (rows, rows, jax.ShapeDtypeStruct((NX, HD, ROWS), F32))
        out_specs = (row, row, block)
    pairs = NX * NX * slots * ROWS * ROWS
    return pl.pallas_call(
        functools.partial(attention_kernel, not state, last, per_x, layout),
        out_shape=out_shape,
        grid_spec=pltpu.PrefetchScalarGridSpec(
            num_scalar_prefetch=1,
            grid=(NX,),
            in_specs=[whole] * (1 + len(pieces)) + [row, row, block][: len(state)],
            out_specs=out_specs,
            scratch_shapes=scratch,
        ),
        compiler_params=params(14),
        cost_estimate=pl.CostEstimate(
            flops=12 * pairs * HD, transcendentals=pairs, bytes_accessed=4 << 20
        ),
        name="attention_last" if last else "attention_pass",
    )(place, in_hbm(own), *[in_hbm(piece) for piece in pieces], *state)


def project_kernel(y_ref, att_ref, w0, w1, w2a, w2b, w3, hidden_ref, bias_ref, gain_ref, shift_ref,
                   mixed_ref, normed_ref):
    y = y_ref[0]
    mixed = hidden_ref[...].astype(F32) + bias_ref[...]
    for k, offset, w_ref in ((0, 0, w0), (1, 0, w1), (2, 0, w2a), (2, 2, w2b), (3, 0, w3)):
        base = ((y - k) & 3) * 4 + offset
        for i in range(w_ref.shape[0]):
            mixed = mixed + jnp.dot(att_ref[base + i, :, :HD], w_ref[i], preferred_element_type=F32)
    mixed_ref[...] = mixed
    mean = jnp.mean(mixed, axis=-1, keepdims=True)
    centered = mixed - mean
    var = jnp.mean(centered * centered, axis=-1, keepdims=True)
    normed = centered * lax.rsqrt(var + EPSILON) * gain_ref[...] + shift_ref[...]
    normed_ref[...] = normed.astype(BF16)


def project(y, attended, weights, hidden, bias, gain, shift):
    rows, width = ROWS // NY, hidden.shape[1]
    full = lambda *shape: pl.BlockSpec(shape, lambda i, t: (0,) * len(shape))
    return pl.pallas_call(
        project_kernel,
        out_shape=(
            jax.ShapeDtypeStruct((rows, width), F32),
            jax.ShapeDtypeStruct((rows, width), BF16),
        ),
        grid_spec=pltpu.PrefetchScalarGridSpec(
            num_scalar_prefetch=1,
            grid=(1,),
            in_specs=[full(16, rows, 128)]
            + [full(*w.shape) for w in weights]
            + [pl.BlockSpec((rows, width), lambda i, t: (t[0], 0))]
            + [full(1, width)] * 3,
            out_specs=(full(rows, width), full(rows, width)),
        ),
        compiler_params=params(16),
        name="project",
    )(y, attended, *weights, hidden, bias, gain, shift)


def mlp_kernel(x0, x1, x2a, x2b, x3, up_ref, bias_ref, down_ref, o0, o1, o2a, o2b, o3, rows, total):
    step = pl.program_id(0)

    @pl.when(step == 0)
    def _():
        at = 0
        for x in (x0, x1, x2a, x2b, x3):
            rows[at : at + x.shape[0]] = x[...]
            at += x.shape[0]

    units = jnp.dot(rows[...], up_ref[...], preferred_element_type=F32) + bias_ref[...]
    units = 0.5 * units * (1.0 + lax.erf(units * float(np.sqrt(0.5))))
    part = jnp.dot(units.astype(BF16), down_ref[...], preferred_element_type=F32)

    @pl.when(step == 0)
    def _():
        total[...] = part

    @pl.when(step > 0)
    def _():
        total[...] += part

    @pl.when(step == pl.num_programs(0) - 1)
    def _():
        at = 0
        for o in (o0, o1, o2a, o2b, o3):
            o[...] = total[at : at + o.shape[0]].astype(o.dtype)
            at += o.shape[0]


def mlp(pieces, up_weight, up_bias, down_weight):
    width, hidden = up_weight.shape
    block = 384
    specs = [pl.BlockSpec(piece.shape, lambda i: (0, 0)) for piece in pieces]
    return pl.pallas_call(
        mlp_kernel,
        out_shape=[
            jax.ShapeDtypeStruct(piece.shape, BF16 if k else F32) for k, piece in enumerate(pieces)
        ],
        grid=(hidden // block,),
        in_specs=specs
        + [
            pl.BlockSpec((width, block), lambda i: (0, i)),
            pl.BlockSpec((1, block), lambda i: (0, i)),
            pl.BlockSpec((block, width), lambda i: (i, 0)),
        ],
        out_specs=specs,
        scratch_shapes=[pltpu.VMEM((ROWS, width), BF16), pltpu.VMEM((ROWS, width), F32)],
        compiler_params=params(16),
        cost_estimate=pl.CostEstimate(
            flops=4 * ROWS * width * hidden,
            transcendentals=ROWS * hidden,
            bytes_accessed=4 * width * hidden,
        ),
        name="mlp",
    )(*pieces, up_weight, up_bias, down_weight)


def merge_kernel(y_ref, x0, x1, x2a, x2b, x3, weight_ref, bias_ref, out_ref, rows, total):
    step = pl.program_id(0)
    size = ROWS // NY
    groups = ROWS // 4

    @pl.when(step == 0)
    def _():
        at = 0
        for x in (x0, x1, x2a, x2b, x3):
            rows[at : at + x.shape[0]] = x[...]
            at += x.shape[0]

    at = lax.broadcasted_iota(jnp.int32, (groups, ROWS), 1)
    group = lax.broadcasted_iota(jnp.int32, (groups, ROWS), 0)
    piece = (at >= size).astype(jnp.int32) + (at >= 2 * size) + (at >= 3 * size)
    row = ((y_ref[0] - piece) & 3) * size + at - piece * size
    pick = (row == 4 * group + step).astype(F32).astype(BF16)
    chosen = jnp.dot(pick, rows[...], preferred_element_type=F32).astype(BF16)
    part = jnp.dot(chosen, weight_ref[...], preferred_element_type=F32)

    @pl.when(step == 0)
    def _():
        total[...] = part

    @pl.when(step > 0)
    def _():
        total[...] += part

    @pl.when(step == pl.num_programs(0) - 1)
    def _():
        out_ref[...] = (total[...] + bias_ref[...]).astype(BF16)


def merge(y, pieces, weight, bias):
    width = pieces[0].shape[1]
    features = weight.shape[1]
    groups = ROWS // 4
    return pl.pallas_call(
        merge_kernel,
        out_shape=jax.ShapeDtypeStruct((groups, features), BF16),
        grid_spec=pltpu.PrefetchScalarGridSpec(
            num_scalar_prefetch=1,
            grid=(4,),
            in_specs=[pl.BlockSpec(piece.shape, lambda i, t: (0, 0)) for piece in pieces]
            + [
                pl.BlockSpec((width, features), lambda i, t: (i, 0)),
                pl.BlockSpec((1, features), lambda i, t: (0, 0)),
            ],
            out_specs=pl.BlockSpec((groups, features), lambda i, t: (0, 0)),
            scratch_shapes=[pltpu.VMEM((ROWS, width), BF16), pltpu.VMEM((groups, features), F32)],
        ),
        compiler_params=params(16),
        name="merge",
    )(y, *pieces, weight, bias)


def body(
    hidden_in,
    queries,
    keys,
    values,
    out_weight,
    out_bias,
    norm_gain,
    norm_bias,
    up_weight,
    up_bias,
    down_weight,
    down_bias,
    merge_weight,
    merge_bias,
    group_segments,
    owner_slots,
):
    heads = 4
    width = hidden_in.shape[1]
    request_total = owner_slots.shape[0]
    x = lax.axis_index("x")
    y = lax.axis_index("y")
    z = lax.axis_index("z")
    y_scalar = jnp.reshape(y, (1,)).astype(jnp.int32)

    swap = [(0, 1), (1, 0)]
    requests = jnp.arange(request_total, dtype=jnp.int32)
    key_parts = keys.T.reshape(heads, HD, ROWS)
    value_parts = values.T.reshape(heads, HD, ROWS)
    query_parts = queries.T.reshape(heads, HD, ROWS)
    marks = jnp.broadcast_to(jnp.repeat(group_segments, 4).astype(BF16), (heads, 8, ROWS))
    parts = jnp.concatenate([key_parts, value_parts, marks, query_parts], axis=1)
    def part_of(k):
        return lax.dynamic_slice_in_dim(parts, (x + k) & 3, 1, 0)

    own_parts = [part_of(0)] + [lax.ppermute(part_of(k), "x", ring(NX, k)) for k in range(1, NX)]
    own = jnp.concatenate(own_parts, axis=0)
    sent = own[:, :QUERY_AT]
    behind, ahead, far_a, far_b = [
        lax.ppermute(value, "z", ring(NZ, k))
        for value, k in ((sent, 1), (sent, NZ - 1), (sent[:2], 2), (sent[2:], 2))
    ]
    own_c = lax.ppermute(sent, "c", swap)
    place = jnp.stack([x, z]).astype(jnp.int32)
    state = attention_pass(place, own, [own, own_c], ((0, 0, 4), (1, 0, 4)), (), False)
    behind, ahead, far_a, far_b, state = lax.optimization_barrier(
        (behind, ahead, far_a, far_b, state)
    )
    pieces = []
    for piece in (behind, ahead, far_a, far_b):
        pieces += [piece, lax.ppermute(piece, "c", swap)]
    layout = ((0, 0, 4), (1, 0, 4), (4, 0, 4), (5, 0, 4), (2, 0, 2), (3, 0, 2), (2, 2, 2), (3, 2, 2))
    attended, row_max = attention_pass(place, own, pieces, layout, state, True)
    row_segments = jnp.take(own[:, MARK_AT], (x - jnp.arange(NX)) & 3, axis=0).astype(jnp.int32)

    attended = lax.all_to_all(attended.reshape(16, ROWS // NY, 128), ("y", "x"), 0, 0)
    weights = [
        w.reshape(w.shape[0] // HD, HD, width) for w in (out_weight,) + shifted(out_weight)
    ]
    mixed, normed = project(
        y_scalar, attended, weights, hidden_in, out_bias[None], norm_gain[None], norm_bias[None]
    )

    down = mlp((normed,) + shifted(normed), in_hbm(up_weight), up_bias[None], in_hbm(down_weight))
    back = [
        lax.ppermute(value, "y", ring(NY, NY - k))
        for value, k in ((down[1], 1), (down[4], 3), (down[2], 2), (down[3], 2))
    ]
    far = jnp.concatenate(back[2:], axis=0)
    state = mixed + down_bias + down[0]
    for value in (back[0], back[1], far):
        state = state + value.astype(F32)
    state_bf = state.astype(BF16)
    state_all = (state_bf,) + shifted(state_bf)
    merged_out = merge(y_scalar, state_all, in_hbm(merge_weight), merge_bias[None])

    member = row_segments[None] == requests[:, None, None]
    request_max = jnp.max(jnp.where(member, row_max[:, 0][None], NEGATIVE), axis=(1, 2))
    request_max = request_max * (HD**-0.5)
    squares = jnp.sum(state * state, axis=-1)
    own_groups = lax.dynamic_slice_in_dim(group_segments, y * (ROWS // 16), ROWS // 16)
    own_rows = jnp.repeat(own_groups, 4)
    sums = jnp.sum(jnp.where(own_rows[None] == requests[:, None], squares[None], 0.0), axis=1)
    chosen = owner_slots[None, :] == jnp.arange(request_total, dtype=jnp.int32)[:, None]
    slot_sums = jnp.sum(jnp.where(chosen, sums[None], 0.0), axis=1)
    slot_max = jnp.sum(jnp.where(chosen, request_max[None], 0.0), axis=1)
    own_counts = jnp.sum((own_rows[None] == requests[:, None]).astype(F32), axis=1)
    slot_counts = jnp.sum(jnp.where(chosen, own_counts[None], 0.0), axis=1)
    sent = [slot_sums, slot_max, slot_counts]
    sent = jnp.concatenate([value.reshape(CHUNKS, 2) for value in sent], axis=1)
    sent = jnp.pad(sent, ((0, 0), (0, 122)))
    sent = jnp.broadcast_to(sent[None], (NY,) + sent.shape).reshape(NY * CHUNKS, 128)
    sent, _ = lax.optimization_barrier((sent, state_all[1]))
    got = lax.all_to_all(sent, ("y", "x", "z", "c"), 0, 0, tiled=True)
    got = got.reshape(NY, NX, NZ * NC, 128)
    own_sums = jnp.sum(got[..., :2], axis=(0, 1, 2))
    own_counts = jnp.sum(got[..., 4:6], axis=(0, 1, 2))
    state_rms = jnp.sqrt(own_sums / (own_counts * width) + EPSILON)
    plane = lax.dynamic_index_in_dim(got[..., 2:4], y, 0, keepdims=False)
    logit_max = jnp.transpose(jnp.max(plane, axis=1))
    return (merged_out, state_rms, logit_max)


def solution(mesh):
    fine = Mesh(mesh.devices.reshape(NY, NX, NZ, NC), ("y", "x", "z", "c"))
    blk = ("x", "z", "c")
    in_specs = (
        P(blk, None),
        P(blk, "y"),
        P(blk, "y"),
        P(blk, "y"),
        P("y", None),
        P(),
        P(),
        P(),
        P(None, "y"),
        P("y"),
        P("y", None),
        P(),
        P(None, "y"),
        P("y"),
        P(blk),
        P(),
    )
    out_specs = (P(blk, "y"), P(blk), P(blk, "y"))
    return jax.shard_map(body, mesh=fine, in_specs=in_specs, out_specs=out_specs, check_vma=False)
```

```python
import functools

import jax
import jax.numpy as jnp
import numpy as np
from jax import lax
from jax.experimental import pallas as pl
from jax.experimental.pallas import tpu as pltpu
from jax.sharding import Mesh
from jax.sharding import PartitionSpec as P

HD = 88
NEGATIVE = -1e30
EPSILON = 1e-06
F32 = jnp.float32
BF16 = jnp.bfloat16

NY, NX, NZ, NC = 4, 4, 4, 2
ROWS = 384
CHUNKS = NX * NZ * NC
REQUESTS = 64
MARK_AT, QUERY_AT = 2 * HD, 2 * HD + 8
EXP2_SCALE = float(np.log2(np.e) / np.sqrt(HD))


def ring(size, shift):
    return [(i, (i + shift) % size) for i in range(size)]


def shifted(value):
    near = [lax.ppermute(value, "y", ring(NY, k)) for k in (1, 3)]
    half = value.shape[0] // 2
    far = [lax.ppermute(part, "y", ring(NY, 2)) for part in (value[:half], value[half:])]
    return near[0], far[0], far[1], near[1]


def in_hbm(value):
    return pltpu.with_memory_space_constraint(value, pltpu.HBM)


def params(mib):
    return pltpu.CompilerParams(vmem_limit_bytes=mib << 20)


def attention_kernel(first, last, per_x, layout, place_ref, *refs):
    count = len(layout)
    own, pieces, refs = refs[0], refs[1 : 1 + count], refs[1 + count :]
    if not first:
        top_in, mass_in, total_in = refs[:3]
        refs = refs[3:]
    if last:
        out_ref, top_ref, mass_at, total_at = refs[:4]
        refs = refs[4:]
    else:
        top_ref, mass_ref, total_ref = refs[:3]
        refs = refs[3:]
        mass_at, total_at = mass_ref.at[0], total_ref.at[0]
    top_at = top_ref.at[0]
    queries, marks, keys, values, key_marks, spread, s0, s1, p0, p1, ends, own_ends, sems = refs
    part = pl.program_id(0)
    x_here, z_here = place_ref[0], place_ref[1]
    steps = NX * per_x

    @pl.when(part == 0)
    def _():
        copies = [(own.at[:, pl.ds(QUERY_AT, HD)], queries), (own.at[:, pl.ds(MARK_AT, 8)], marks)]
        for piece, (slot, at, size) in zip(pieces, layout):
            at = pl.ds(at, size)
            copies.append((piece.at[:, pl.ds(0, HD)], keys.at[slot, at]))
            copies.append((piece.at[:, pl.ds(HD, HD)], values.at[slot, at]))
            copies.append((piece.at[:, pl.ds(MARK_AT, 8)], key_marks.at[slot, at]))
        copies = [pltpu.make_async_copy(*c, sems.at[i]) for i, c in enumerate(copies)]
        for copy in copies:
            copy.start()
        for copy in copies:
            copy.wait()
        for k in range(NX):
            mark = marks[k][:1].astype(F32)
            own_ends[k, 0] = jnp.min(mark)
            own_ends[k, 1] = jnp.max(mark)
            for pair in range(per_x):
                even = key_marks[2 * pair, k][:1].astype(F32)
                odd = key_marks[2 * pair + 1, k][:1].astype(F32)
                ends[pair, k, 0] = jnp.min(jnp.minimum(even, odd))
                ends[pair, k, 1] = jnp.max(jnp.maximum(even, odd))

    def locate(t):
        if per_x == 1:
            return 0, (x_here - t) & 3
        x_of = t // per_x
        z_of = t - x_of * per_x
        z_of = z_of + (z_of >= z_here).astype(jnp.int32)
        return ((z_here - z_of) & 3) - 1, (x_here - x_of) & 3

    here = (x_here - part) & 3
    mark = marks[here][:1].astype(F32)
    q_first, q_last = own_ends[here, 0], own_ends[here, 1]
    requests = lax.broadcasted_iota(jnp.int32, (REQUESTS, ROWS), 0).astype(F32)
    spread[...] = jnp.where(requests == mark, 1.0, 0.0).astype(BF16)
    low, high = jnp.int32(steps), jnp.int32(0)
    for t in range(steps):
        pair, at = locate(jnp.int32(t))
        active = (ends[pair, at, 1] >= q_first) & (ends[pair, at, 0] <= q_last)
        low = jnp.where(active & (low == steps), t, low)
        high = jnp.where(active, t + 1, high)

    if first:
        top_at[...] = jnp.full((1, ROWS), NEGATIVE, F32)
        mass_at[...] = jnp.zeros((1, ROWS), F32)
        total_at[...] = jnp.zeros((HD, ROWS), F32)
    else:
        top_at[...] = top_in[0]
        mass_at[...] = mass_in[0]
        total_at[...] = total_in[0]

    def both(a, b):
        return lax.dot_general(a, b, (((0,), (0,)), ((), ())), preferred_element_type=F32)

    def score(slot, at, scores):
        scores[...] = both(keys[slot, at], queries[here])

    def gather(slot, at, weights, factor):
        total_at[...] = total_at[...] * factor + jnp.dot(
            values[slot, at], weights[...], preferred_element_type=F32
        )

    def soften(slot, at, scores, weights, top, mass, masked):
        s = scores[...]
        if masked:
            key_mark = key_marks[slot, at][:1].astype(F32)
            key_spread = jnp.where(requests == key_mark, 1.0, 0.0).astype(BF16)
            s = jnp.where(both(key_spread, spread[...]) > 0.5, s, NEGATIVE)
        new_top = jnp.maximum(top, jnp.max(s, axis=0, keepdims=True))
        exponents = jnp.exp2((s - new_top) * EXP2_SCALE)
        factor = jnp.exp2((top - new_top) * EXP2_SCALE)
        weights[...] = exponents.astype(BF16)
        return new_top, mass * factor + jnp.sum(exponents, axis=0, keepdims=True), factor

    def step(t, pair, at, carried, masked):
        top, mass, factor = carried
        old_pair, old_at = locate(jnp.maximum(t - 1, 0))
        new_pair, new_at = locate(jnp.minimum(t + 1, steps - 1))
        score(2 * pair + 1, at, s1)
        gather(2 * old_pair + 1, old_at, p1, factor)
        top, mass, factor = soften(2 * pair, at, s0, p0, top, mass, masked)
        score(2 * new_pair, new_at, s0)
        gather(2 * pair, at, p0, factor)
        return soften(2 * pair + 1, at, s1, p1, top, mass, masked)

    def one_pair(t, carried):
        pair, at = locate(t)
        full = (q_first == q_last) & (ends[pair, at, 0] == q_first) & (ends[pair, at, 1] == q_first)
        return lax.cond(
            full,
            lambda c: step(t, pair, at, c, False),
            lambda c: step(t, pair, at, c, True),
            carried,
        )

    @pl.when(high > low)
    def _():
        p1[...] = jnp.zeros_like(p1)
        pair, at = locate(low)
        score(2 * pair, at, s0)
        start = (top_at[...], mass_at[...], jnp.ones((1, ROWS), F32))
        top, mass, factor = lax.fori_loop(low, high, one_pair, start)
        pair, at = locate(high - 1)
        gather(2 * pair + 1, at, p1, factor)
        top_at[...] = top
        mass_at[...] = mass

    if last:
        attended = jnp.transpose(total_at[...] / mass_at[...]).astype(BF16)
        for y in range(NY):
            out_ref[y, 0, :, :HD] = attended[y * 96 : (y + 1) * 96]


def attention_pass(place, own, pieces, layout, state, last):
    per_x = 3 if state else 1
    slots = 2 * per_x
    whole = pl.BlockSpec(memory_space=pltpu.HBM)
    row = pl.BlockSpec((1, 1, ROWS), lambda i, t: (i, 0, 0))
    block = pl.BlockSpec((1, HD, ROWS), lambda i, t: (i, 0, 0))
    rows = jax.ShapeDtypeStruct((NX, 1, ROWS), F32)
    scratch = [
        pltpu.VMEM((NX, HD, ROWS), BF16),
        pltpu.VMEM((NX, 8, ROWS), BF16),
        pltpu.VMEM((slots, NX, HD, ROWS), BF16),
        pltpu.VMEM((slots, NX, HD, ROWS), BF16),
        pltpu.VMEM((slots, NX, 8, ROWS), BF16),
        pltpu.VMEM((REQUESTS, ROWS), BF16),
        pltpu.VMEM((ROWS, ROWS), F32),
        pltpu.VMEM((ROWS, ROWS), F32),
        pltpu.VMEM((ROWS, ROWS), BF16),
        pltpu.VMEM((ROWS, ROWS), BF16),
        pltpu.SMEM((per_x, NX, 2), F32),
        pltpu.SMEM((NX, 2), F32),
        pltpu.SemaphoreType.DMA((2 + 3 * len(layout),)),
    ]
    if last:
        out_shape = (jax.ShapeDtypeStruct((NY, NX, ROWS // NY, 128), BF16), rows)
        out_specs = (pl.BlockSpec((NY, 1, ROWS // NY, 128), lambda i, t: (0, i, 0, 0)), row)
        scratch = [pltpu.VMEM((1, ROWS), F32), pltpu.VMEM((HD, ROWS), F32)] + scratch
    else:
        out_shape = (rows, rows, jax.ShapeDtypeStruct((NX, HD, ROWS), F32))
        out_specs = (row, row, block)
    pairs = NX * NX * slots * ROWS * ROWS
    return pl.pallas_call(
        functools.partial(attention_kernel, not state, last, per_x, layout),
        out_shape=out_shape,
        grid_spec=pltpu.PrefetchScalarGridSpec(
            num_scalar_prefetch=1,
            grid=(NX,),
            in_specs=[whole] * (1 + len(pieces)) + [row, row, block][: len(state)],
            out_specs=out_specs,
            scratch_shapes=scratch,
        ),
        compiler_params=params(14),
        cost_estimate=pl.CostEstimate(
            flops=12 * pairs * HD, transcendentals=pairs, bytes_accessed=4 << 20
        ),
        name="attention_last" if last else "attention_pass",
    )(place, in_hbm(own), *[in_hbm(piece) for piece in pieces], *state)


def bring_near_kernel(after, *refs):
    count = len(refs) // 2
    sources, targets, sems = refs[:count], refs[count : 2 * count], refs[2 * count]
    copies = []
    for i, (source, target) in enumerate(zip(sources, targets)):
        size = source.shape[0] // 4
        for j in range(4):
            at = pl.ds(j * size, size)
            copies.append(pltpu.make_async_copy(source.at[at], target.at[at], sems.at[4 * i + j]))
    for copy in copies:
        copy.start()
    for copy in copies:
        copy.wait()


def bring_near(after, *weights):
    whole = pl.BlockSpec(memory_space=pltpu.HBM)
    return pl.pallas_call(
        bring_near_kernel,
        out_shape=[pltpu.VMEM(w.shape, w.dtype) for w in weights],
        in_specs=[pl.BlockSpec(memory_space=pl.ANY)] + [whole] * len(weights),
        out_specs=[pl.BlockSpec(memory_space=pltpu.VMEM)] * len(weights),
        scratch_shapes=[pltpu.SemaphoreType.DMA((4 * len(weights),))],
        compiler_params=params(8),
        cost_estimate=pl.CostEstimate(flops=0, transcendentals=0, bytes_accessed=10 << 20),
        name="bring_near",
    )(after, *[in_hbm(w) for w in weights])


def project_kernel(y_ref, att_ref, w_ref, hidden_ref, bias_ref, gain_ref, shift_ref,
                   mixed_ref, normed_ref):
    mixed = hidden_ref[...].astype(F32) + bias_ref[...]
    for head in range(16):
        mixed = mixed + jnp.dot(att_ref[head, :, :HD], w_ref[head], preferred_element_type=F32)
    mixed_ref[...] = mixed
    mean = jnp.mean(mixed, axis=-1, keepdims=True)
    centered = mixed - mean
    var = jnp.mean(centered * centered, axis=-1, keepdims=True)
    normed = centered * lax.rsqrt(var + EPSILON) * gain_ref[...] + shift_ref[...]
    normed_ref[...] = normed.astype(BF16)


def project(y, attended, weights, hidden, bias, gain, shift):
    rows, width = ROWS // NY, hidden.shape[1]
    full = lambda *shape: pl.BlockSpec(shape, lambda i, t: (0,) * len(shape))
    return pl.pallas_call(
        project_kernel,
        out_shape=(
            jax.ShapeDtypeStruct((rows, width), F32),
            jax.ShapeDtypeStruct((rows, width), BF16),
        ),
        grid_spec=pltpu.PrefetchScalarGridSpec(
            num_scalar_prefetch=1,
            grid=(1,),
            in_specs=[full(16, rows, 128)]
            + [full(16, HD, width)]
            + [pl.BlockSpec((rows, width), lambda i, t: (t[0], 0))]
            + [full(1, width)] * 3,
            out_specs=(full(rows, width), full(rows, width)),
        ),
        compiler_params=params(16),
        name="project",
    )(y, attended, weights, hidden, bias, gain, shift)


def mlp_kernel(x0, x1, x2a, x2b, x3, up_ref, bias_ref, down_ref, o0, o1, o2a, o2b, o3, rows, total):
    at = 0
    for x in (x0, x1, x2a, x2b, x3):
        rows[at : at + x.shape[0]] = x[...]
        at += x.shape[0]
    block = 384
    for step in range(up_ref.shape[1] // block):
        part = slice(step * block, (step + 1) * block)
        units = jnp.dot(rows[...], up_ref[:, part], preferred_element_type=F32) + bias_ref[:, part]
        units = 0.5 * units * (1.0 + lax.erf(units * float(np.sqrt(0.5))))
        down = jnp.dot(units.astype(BF16), down_ref[part], preferred_element_type=F32)
        total[...] = down if step == 0 else total[...] + down
    at = 0
    for o in (o0, o1, o2a, o2b, o3):
        o[...] = total[at : at + o.shape[0]].astype(o.dtype)
        at += o.shape[0]


def mlp(pieces, up_weight, up_bias, down_weight):
    width, hidden = up_weight.shape
    near = pl.BlockSpec(memory_space=pltpu.VMEM)
    return pl.pallas_call(
        mlp_kernel,
        out_shape=[
            jax.ShapeDtypeStruct(piece.shape, BF16 if k else F32) for k, piece in enumerate(pieces)
        ],
        in_specs=[near] * (len(pieces) + 3),
        out_specs=[near] * len(pieces),
        scratch_shapes=[pltpu.VMEM((ROWS, width), BF16), pltpu.VMEM((ROWS, width), F32)],
        compiler_params=params(12),
        cost_estimate=pl.CostEstimate(
            flops=4 * ROWS * width * hidden,
            transcendentals=ROWS * hidden,
            bytes_accessed=4 * width * hidden,
        ),
        name="mlp",
    )(*pieces, up_weight, up_bias, down_weight)


def merge_kernel(y_ref, x0, x1, x2a, x2b, x3, weight_ref, bias_ref, out_ref, rows):
    size = ROWS // NY
    groups = ROWS // 4
    width = rows.shape[1]
    at = 0
    for x in (x0, x1, x2a, x2b, x3):
        rows[at : at + x.shape[0]] = x[...]
        at += x.shape[0]
    at = lax.broadcasted_iota(jnp.int32, (groups, ROWS), 1)
    group = lax.broadcasted_iota(jnp.int32, (groups, ROWS), 0)
    piece = (at >= size).astype(jnp.int32) + (at >= 2 * size) + (at >= 3 * size)
    row = ((y_ref[0] - piece) & 3) * size + at - piece * size
    total = bias_ref[...]
    for member in range(4):
        pick = (row == 4 * group + member).astype(F32).astype(BF16)
        chosen = jnp.dot(pick, rows[...], preferred_element_type=F32).astype(BF16)
        weight = weight_ref[member * width : (member + 1) * width]
        total = total + jnp.dot(chosen, weight, preferred_element_type=F32)
    out_ref[...] = total.astype(BF16)


def merge(y, pieces, weight, bias):
    near = pl.BlockSpec(memory_space=pltpu.VMEM)
    return pl.pallas_call(
        merge_kernel,
        out_shape=jax.ShapeDtypeStruct((ROWS // 4, weight.shape[1]), BF16),
        in_specs=[pl.BlockSpec(memory_space=pltpu.SMEM)] + [near] * (len(pieces) + 2),
        out_specs=near,
        scratch_shapes=[pltpu.VMEM((ROWS, pieces[0].shape[1]), BF16)],
        compiler_params=params(12),
        name="merge",
    )(y, *pieces, weight, bias)


def body(
    hidden_in,
    queries,
    keys,
    values,
    out_weight,
    out_bias,
    norm_gain,
    norm_bias,
    up_weight,
    up_bias,
    down_weight,
    down_bias,
    merge_weight,
    merge_bias,
    group_segments,
    owner_slots,
):
    heads = 4
    width = hidden_in.shape[1]
    request_total = owner_slots.shape[0]
    x = lax.axis_index("x")
    y = lax.axis_index("y")
    z = lax.axis_index("z")
    y_scalar = jnp.reshape(y, (1,)).astype(jnp.int32)

    swap = [(0, 1), (1, 0)]
    requests = jnp.arange(request_total, dtype=jnp.int32)
    key_parts = keys.T.reshape(heads, HD, ROWS)
    value_parts = values.T.reshape(heads, HD, ROWS)
    query_parts = queries.T.reshape(heads, HD, ROWS)
    marks = jnp.broadcast_to(jnp.repeat(group_segments, 4).astype(BF16), (heads, 8, ROWS))
    parts = jnp.concatenate([key_parts, value_parts, marks, query_parts], axis=1)
    def part_of(k):
        return lax.dynamic_slice_in_dim(parts, (x + k) & 3, 1, 0)

    own_parts = [part_of(0)] + [lax.ppermute(part_of(k), "x", ring(NX, k)) for k in range(1, NX)]
    own = jnp.concatenate(own_parts, axis=0)
    sent = own[:, :QUERY_AT]
    behind, ahead, far_a, far_b = [
        lax.ppermute(value, "z", ring(NZ, k))
        for value, k in ((sent, 1), (sent, NZ - 1), (sent[:2], 2), (sent[2:], 2))
    ]
    own_c = lax.ppermute(sent, "c", swap)
    place = jnp.stack([x, z]).astype(jnp.int32)
    state = attention_pass(place, own, [own, own_c], ((0, 0, 4), (1, 0, 4)), (), False)
    behind, ahead, far_a, far_b, state = lax.optimization_barrier(
        (behind, ahead, far_a, far_b, state)
    )
    pieces = []
    for piece in (behind, ahead, far_a, far_b):
        pieces += [piece, lax.ppermute(piece, "c", swap)]
    layout = ((0, 0, 4), (1, 0, 4), (4, 0, 4), (5, 0, 4), (2, 0, 2), (3, 0, 2), (2, 2, 2), (3, 2, 2))
    attended, row_max = attention_pass(place, own, pieces, layout, state, True)
    row_segments = jnp.take(own[:, MARK_AT], (x - jnp.arange(NX)) & 3, axis=0).astype(jnp.int32)

    up_near, down_near = bring_near(row_max, up_weight, down_weight)
    attended = lax.all_to_all(attended.reshape(16, ROWS // NY, 128), ("y", "x"), 0, 0)
    weights = lax.all_gather(out_weight, "y", axis=0, tiled=True).reshape(16, HD, width)
    mixed, normed = project(
        y_scalar, attended, in_hbm(weights), hidden_in, out_bias[None], norm_gain[None], norm_bias[None]
    )

    down = mlp((normed,) + shifted(normed), up_near, up_bias[None], down_near)
    (merge_near,) = bring_near(down[0], merge_weight)
    back = [
        lax.ppermute(value, "y", ring(NY, NY - k))
        for value, k in ((down[1], 1), (down[4], 3), (down[2], 2), (down[3], 2))
    ]
    far = jnp.concatenate(back[2:], axis=0)
    state = mixed + down_bias + down[0]
    for value in (back[0], back[1], far):
        state = state + value.astype(F32)
    state_bf = state.astype(BF16)
    state_all = (state_bf,) + shifted(state_bf)
    merged_out = merge(y_scalar, state_all, merge_near, merge_bias[None])

    member = row_segments[None] == requests[:, None, None]
    request_max = jnp.max(jnp.where(member, row_max[:, 0][None], NEGATIVE), axis=(1, 2))
    request_max = request_max * (HD**-0.5)
    own_groups = lax.dynamic_slice_in_dim(group_segments, y * (ROWS // 16), ROWS // 16)
    own_rows = jnp.repeat(own_groups, 4)
    mine = own_rows[None] == requests[:, None]
    own_counts = jnp.sum(mine.astype(F32), axis=1)
    row_slots = jnp.sum(jnp.where(mine, owner_slots[:, None], 0), axis=0)
    lane = lax.broadcasted_iota(jnp.int32, (CHUNKS, 128), 1)
    owner = lax.broadcasted_iota(jnp.int32, (CHUNKS, 128), 0)
    slot = 2 * owner + (lane & 1)
    facts = jnp.where(lane[None] < 4, request_max[:, None, None], own_counts[:, None, None])
    facts = jnp.sum(jnp.where(owner_slots[:, None, None] == slot[None], facts, 0.0), axis=0)
    squares = jnp.sum(state * state, axis=-1)
    sums = jnp.where(row_slots[:, None, None] == slot[None], squares[:, None, None], 0.0)
    sent = jnp.where(lane < 2, jnp.sum(sums, axis=0), facts)
    sent = jnp.broadcast_to(sent[None], (NY,) + sent.shape).reshape(NY * CHUNKS, 128)
    got = lax.all_to_all(sent, ("y", "x", "z", "c"), 0, 0, tiled=True)
    got = got.reshape(NY, NX, NZ * NC, 128)
    own_sums = jnp.sum(got[..., :2], axis=(0, 1, 2))
    own_counts = jnp.sum(got[..., 4:6], axis=(0, 1, 2))
    state_rms = jnp.sqrt(own_sums / (own_counts * width) + EPSILON)
    plane = lax.dynamic_index_in_dim(got[..., 2:4], y, 0, keepdims=False)
    logit_max = jnp.transpose(jnp.max(plane, axis=1))
    return (merged_out, state_rms, logit_max)


def solution(mesh):
    fine = Mesh(mesh.devices.reshape(NY, NX, NZ, NC), ("y", "x", "z", "c"))
    blk = ("x", "z", "c")
    in_specs = (
        P(blk, None),
        P(blk, "y"),
        P(blk, "y"),
        P(blk, "y"),
        P("y", None),
        P(),
        P(),
        P(),
        P(None, "y"),
        P("y"),
        P("y", None),
        P(),
        P(None, "y"),
        P("y"),
        P(blk),
        P(),
    )
    out_specs = (P(blk, "y"), P(blk), P(blk, "y"))
    return jax.shard_map(body, mesh=fine, in_specs=in_specs, out_specs=out_specs, check_vma=False)
```

```python
import functools

import jax
import jax.numpy as jnp
import numpy as np
from jax import lax
from jax.experimental import pallas as pl
from jax.experimental.pallas import tpu as pltpu
from jax.sharding import Mesh
from jax.sharding import PartitionSpec as P

HD = 88
NEGATIVE = -1e30
EPSILON = 1e-06
F32 = jnp.float32
BF16 = jnp.bfloat16

NY, NX, NZ, NC = 4, 4, 4, 2
ROWS = 384
CHUNKS = NX * NZ * NC
REQUESTS = 64
MARK_AT, QUERY_AT = 2 * HD, 2 * HD + 8
EXP2_SCALE = float(np.log2(np.e) / np.sqrt(HD))


def ring(size, shift):
    return [(i, (i + shift) % size) for i in range(size)]


def shifted(value):
    near = [lax.ppermute(value, "y", ring(NY, k)) for k in (1, 3)]
    half = value.shape[0] // 2
    far = [lax.ppermute(part, "y", ring(NY, 2)) for part in (value[:half], value[half:])]
    return near[0], far[0], far[1], near[1]


def in_hbm(value):
    return pltpu.with_memory_space_constraint(value, pltpu.HBM)


def params(mib):
    return pltpu.CompilerParams(vmem_limit_bytes=mib << 20)


def attention_kernel(first, last, per_x, layout, place_ref, *refs):
    count = len(layout)
    own, pieces, refs = refs[0], refs[1 : 1 + count], refs[1 + count :]
    if not first:
        top_in, mass_in, total_in = refs[:3]
        refs = refs[3:]
    if last:
        out_ref, top_ref, mass_at, total_at = refs[:4]
        refs = refs[4:]
    else:
        top_ref, mass_ref, total_ref = refs[:3]
        refs = refs[3:]
        mass_at, total_at = mass_ref.at[0], total_ref.at[0]
    top_at = top_ref.at[0]
    queries, marks, keys, values, key_marks, spread, s0, s1, p0, p1, ends, own_ends, sems = refs
    part = pl.program_id(0)
    x_here, z_here = place_ref[0], place_ref[1]
    steps = NX * per_x

    @pl.when(part == 0)
    def _():
        copies = [(own.at[:, pl.ds(QUERY_AT, HD)], queries), (own.at[:, pl.ds(MARK_AT, 8)], marks)]
        for piece, (slot, at, size) in zip(pieces, layout):
            at = pl.ds(at, size)
            copies.append((piece.at[:, pl.ds(0, HD)], keys.at[slot, at]))
            copies.append((piece.at[:, pl.ds(HD, HD)], values.at[slot, at]))
            copies.append((piece.at[:, pl.ds(MARK_AT, 8)], key_marks.at[slot, at]))
        copies = [pltpu.make_async_copy(*c, sems.at[i]) for i, c in enumerate(copies)]
        for copy in copies:
            copy.start()
        for copy in copies:
            copy.wait()
        for k in range(NX):
            mark = marks[k][:1].astype(F32)
            own_ends[k, 0] = jnp.min(mark)
            own_ends[k, 1] = jnp.max(mark)
            for pair in range(per_x):
                even = key_marks[2 * pair, k][:1].astype(F32)
                odd = key_marks[2 * pair + 1, k][:1].astype(F32)
                ends[pair, k, 0] = jnp.min(jnp.minimum(even, odd))
                ends[pair, k, 1] = jnp.max(jnp.maximum(even, odd))

    def locate(t):
        if per_x == 1:
            return 0, (x_here - t) & 3
        x_of = t // per_x
        z_of = t - x_of * per_x
        z_of = z_of + (z_of >= z_here).astype(jnp.int32)
        return ((z_here - z_of) & 3) - 1, (x_here - x_of) & 3

    here = (x_here - part) & 3
    mark = marks[here][:1].astype(F32)
    q_first, q_last = own_ends[here, 0], own_ends[here, 1]
    requests = lax.broadcasted_iota(jnp.int32, (REQUESTS, ROWS), 0).astype(F32)
    spread[...] = jnp.where(requests == mark, 1.0, 0.0).astype(BF16)
    low, high = jnp.int32(steps), jnp.int32(0)
    for t in range(steps):
        pair, at = locate(jnp.int32(t))
        active = (ends[pair, at, 1] >= q_first) & (ends[pair, at, 0] <= q_last)
        low = jnp.where(active & (low == steps), t, low)
        high = jnp.where(active, t + 1, high)

    if first:
        top_at[...] = jnp.full((1, ROWS), NEGATIVE, F32)
        mass_at[...] = jnp.zeros((1, ROWS), F32)
        total_at[...] = jnp.zeros((HD, ROWS), F32)
    else:
        top_at[...] = top_in[0]
        mass_at[...] = mass_in[0]
        total_at[...] = total_in[0]

    def both(a, b):
        return lax.dot_general(a, b, (((0,), (0,)), ((), ())), preferred_element_type=F32)

    def score(slot, at, scores):
        scores[...] = both(keys[slot, at], queries[here])

    def gather(slot, at, weights, factor):
        total_at[...] = total_at[...] * factor + jnp.dot(
            values[slot, at], weights[...], preferred_element_type=F32
        )

    def soften(slot, at, scores, weights, top, mass, masked):
        s = scores[...]
        if masked:
            key_mark = key_marks[slot, at][:1].astype(F32)
            key_spread = jnp.where(requests == key_mark, 1.0, 0.0).astype(BF16)
            s = jnp.where(both(key_spread, spread[...]) > 0.5, s, NEGATIVE)
        new_top = jnp.maximum(top, jnp.max(s, axis=0, keepdims=True))
        exponents = jnp.exp2((s - new_top) * EXP2_SCALE)
        factor = jnp.exp2((top - new_top) * EXP2_SCALE)
        weights[...] = exponents.astype(BF16)
        return new_top, mass * factor + jnp.sum(exponents, axis=0, keepdims=True), factor

    def step(t, pair, at, carried, masked):
        top, mass, factor = carried
        old_pair, old_at = locate(jnp.maximum(t - 1, 0))
        new_pair, new_at = locate(jnp.minimum(t + 1, steps - 1))
        score(2 * pair + 1, at, s1)
        gather(2 * old_pair + 1, old_at, p1, factor)
        top, mass, factor = soften(2 * pair, at, s0, p0, top, mass, masked)
        score(2 * new_pair, new_at, s0)
        gather(2 * pair, at, p0, factor)
        return soften(2 * pair + 1, at, s1, p1, top, mass, masked)

    def one_pair(t, carried):
        pair, at = locate(t)
        full = (q_first == q_last) & (ends[pair, at, 0] == q_first) & (ends[pair, at, 1] == q_first)
        return lax.cond(
            full,
            lambda c: step(t, pair, at, c, False),
            lambda c: step(t, pair, at, c, True),
            carried,
        )

    @pl.when(high > low)
    def _():
        p1[...] = jnp.zeros_like(p1)
        pair, at = locate(low)
        score(2 * pair, at, s0)
        start = (top_at[...], mass_at[...], jnp.ones((1, ROWS), F32))
        top, mass, factor = lax.fori_loop(low, high, one_pair, start)
        pair, at = locate(high - 1)
        gather(2 * pair + 1, at, p1, factor)
        top_at[...] = top
        mass_at[...] = mass

    if last:
        attended = jnp.transpose(total_at[...] / mass_at[...]).astype(BF16)
        for y in range(NY):
            out_ref[y, 0, :, :HD] = attended[y * 96 : (y + 1) * 96]


def attention_pass(place, own, pieces, layout, state, last):
    per_x = 3 if state else 1
    slots = 2 * per_x
    whole = pl.BlockSpec(memory_space=pltpu.HBM)
    row = pl.BlockSpec((1, 1, ROWS), lambda i, t: (i, 0, 0))
    block = pl.BlockSpec((1, HD, ROWS), lambda i, t: (i, 0, 0))
    rows = jax.ShapeDtypeStruct((NX, 1, ROWS), F32)
    scratch = [
        pltpu.VMEM((NX, HD, ROWS), BF16),
        pltpu.VMEM((NX, 8, ROWS), BF16),
        pltpu.VMEM((slots, NX, HD, ROWS), BF16),
        pltpu.VMEM((slots, NX, HD, ROWS), BF16),
        pltpu.VMEM((slots, NX, 8, ROWS), BF16),
        pltpu.VMEM((REQUESTS, ROWS), BF16),
        pltpu.VMEM((ROWS, ROWS), F32),
        pltpu.VMEM((ROWS, ROWS), F32),
        pltpu.VMEM((ROWS, ROWS), BF16),
        pltpu.VMEM((ROWS, ROWS), BF16),
        pltpu.SMEM((per_x, NX, 2), F32),
        pltpu.SMEM((NX, 2), F32),
        pltpu.SemaphoreType.DMA((2 + 3 * len(layout),)),
    ]
    if last:
        out_shape = (jax.ShapeDtypeStruct((NY, NX, ROWS // NY, 128), BF16), rows)
        out_specs = (pl.BlockSpec((NY, 1, ROWS // NY, 128), lambda i, t: (0, i, 0, 0)), row)
        scratch = [pltpu.VMEM((1, ROWS), F32), pltpu.VMEM((HD, ROWS), F32)] + scratch
    else:
        out_shape = (rows, rows, jax.ShapeDtypeStruct((NX, HD, ROWS), F32))
        out_specs = (row, row, block)
    pairs = NX * NX * slots * ROWS * ROWS
    return pl.pallas_call(
        functools.partial(attention_kernel, not state, last, per_x, layout),
        out_shape=out_shape,
        grid_spec=pltpu.PrefetchScalarGridSpec(
            num_scalar_prefetch=1,
            grid=(NX,),
            in_specs=[whole] * (1 + len(pieces)) + [row, row, block][: len(state)],
            out_specs=out_specs,
            scratch_shapes=scratch,
        ),
        compiler_params=params(14),
        cost_estimate=pl.CostEstimate(
            flops=12 * pairs * HD, transcendentals=pairs, bytes_accessed=4 << 20
        ),
        name="attention_last" if last else "attention_pass",
    )(place, in_hbm(own), *[in_hbm(piece) for piece in pieces], *state)


def bring_near_kernel(after, *refs):
    count = len(refs) // 2
    sources, targets, sems = refs[:count], refs[count : 2 * count], refs[2 * count]
    copies = []
    for i, (source, target) in enumerate(zip(sources, targets)):
        size = source.shape[0] // 4
        for j in range(4):
            at = pl.ds(j * size, size)
            copies.append(pltpu.make_async_copy(source.at[at], target.at[at], sems.at[4 * i + j]))
    for copy in copies:
        copy.start()
    for copy in copies:
        copy.wait()


def bring_near(after, *weights):
    whole = pl.BlockSpec(memory_space=pltpu.HBM)
    return pl.pallas_call(
        bring_near_kernel,
        out_shape=[pltpu.VMEM(w.shape, w.dtype) for w in weights],
        in_specs=[pl.BlockSpec(memory_space=pl.ANY)] + [whole] * len(weights),
        out_specs=[pl.BlockSpec(memory_space=pltpu.VMEM)] * len(weights),
        scratch_shapes=[pltpu.SemaphoreType.DMA((4 * len(weights),))],
        compiler_params=params(8),
        cost_estimate=pl.CostEstimate(flops=0, transcendentals=0, bytes_accessed=10 << 20),
        name="bring_near",
    )(after, *[in_hbm(w) for w in weights])


def project_kernel(y_ref, att_ref, w0, w1, w2a, w2b, w3, hidden_ref, bias_ref, gain_ref, shift_ref,
                   mixed_ref, normed_ref):
    y = y_ref[0]
    mixed = hidden_ref[...].astype(F32) + bias_ref[...]
    for k, offset, w_ref in ((0, 0, w0), (1, 0, w1), (2, 0, w2a), (2, 2, w2b), (3, 0, w3)):
        base = ((y - k) & 3) * 4 + offset
        for i in range(w_ref.shape[0]):
            mixed = mixed + jnp.dot(att_ref[base + i, :, :HD], w_ref[i], preferred_element_type=F32)
    mixed_ref[...] = mixed
    mean = jnp.mean(mixed, axis=-1, keepdims=True)
    centered = mixed - mean
    var = jnp.mean(centered * centered, axis=-1, keepdims=True)
    normed = centered * lax.rsqrt(var + EPSILON) * gain_ref[...] + shift_ref[...]
    normed_ref[...] = normed.astype(BF16)


def project(y, attended, weights, hidden, bias, gain, shift):
    rows, width = ROWS // NY, hidden.shape[1]
    full = lambda *shape: pl.BlockSpec(shape, lambda i, t: (0,) * len(shape))
    return pl.pallas_call(
        project_kernel,
        out_shape=(
            jax.ShapeDtypeStruct((rows, width), F32),
            jax.ShapeDtypeStruct((rows, width), BF16),
        ),
        grid_spec=pltpu.PrefetchScalarGridSpec(
            num_scalar_prefetch=1,
            grid=(1,),
            in_specs=[full(16, rows, 128)]
            + [full(*w.shape) for w in weights]
            + [pl.BlockSpec((rows, width), lambda i, t: (t[0], 0))]
            + [full(1, width)] * 3,
            out_specs=(full(rows, width), full(rows, width)),
        ),
        compiler_params=params(16),
        name="project",
    )(y, attended, *weights, hidden, bias, gain, shift)


def mlp_kernel(x0, x1, x2a, x2b, x3, up_ref, bias_ref, down_ref, o0, o1, o2a, o2b, o3, rows, total):
    at = 0
    for x in (x0, x1, x2a, x2b, x3):
        rows[at : at + x.shape[0]] = x[...]
        at += x.shape[0]
    block = 384
    for step in range(up_ref.shape[1] // block):
        part = slice(step * block, (step + 1) * block)
        units = jnp.dot(rows[...], up_ref[:, part], preferred_element_type=F32) + bias_ref[:, part]
        units = 0.5 * units * (1.0 + lax.erf(units * float(np.sqrt(0.5))))
        down = jnp.dot(units.astype(BF16), down_ref[part], preferred_element_type=F32)
        total[...] = down if step == 0 else total[...] + down
    at = 0
    for o in (o0, o1, o2a, o2b, o3):
        o[...] = total[at : at + o.shape[0]].astype(o.dtype)
        at += o.shape[0]


def mlp(pieces, up_weight, up_bias, down_weight):
    width, hidden = up_weight.shape
    near = pl.BlockSpec(memory_space=pltpu.VMEM)
    return pl.pallas_call(
        mlp_kernel,
        out_shape=[
            jax.ShapeDtypeStruct(piece.shape, BF16 if k else F32) for k, piece in enumerate(pieces)
        ],
        in_specs=[near] * (len(pieces) + 3),
        out_specs=[near] * len(pieces),
        scratch_shapes=[pltpu.VMEM((ROWS, width), BF16), pltpu.VMEM((ROWS, width), F32)],
        compiler_params=params(12),
        cost_estimate=pl.CostEstimate(
            flops=4 * ROWS * width * hidden,
            transcendentals=ROWS * hidden,
            bytes_accessed=4 * width * hidden,
        ),
        name="mlp",
    )(*pieces, up_weight, up_bias, down_weight)


def merge_kernel(y_ref, x0, x1, x2a, x2b, x3, weight_ref, bias_ref, out_ref, rows):
    size = ROWS // NY
    groups = ROWS // 4
    width = rows.shape[1]
    at = 0
    for x in (x0, x1, x2a, x2b, x3):
        rows[at : at + x.shape[0]] = x[...]
        at += x.shape[0]
    at = lax.broadcasted_iota(jnp.int32, (groups, ROWS), 1)
    group = lax.broadcasted_iota(jnp.int32, (groups, ROWS), 0)
    piece = (at >= size).astype(jnp.int32) + (at >= 2 * size) + (at >= 3 * size)
    row = ((y_ref[0] - piece) & 3) * size + at - piece * size
    total = bias_ref[...]
    for member in range(4):
        pick = (row == 4 * group + member).astype(F32).astype(BF16)
        chosen = jnp.dot(pick, rows[...], preferred_element_type=F32).astype(BF16)
        weight = weight_ref[member * width : (member + 1) * width]
        total = total + jnp.dot(chosen, weight, preferred_element_type=F32)
    out_ref[...] = total.astype(BF16)


def merge(y, pieces, weight, bias):
    near = pl.BlockSpec(memory_space=pltpu.VMEM)
    return pl.pallas_call(
        merge_kernel,
        out_shape=jax.ShapeDtypeStruct((ROWS // 4, weight.shape[1]), BF16),
        in_specs=[pl.BlockSpec(memory_space=pltpu.SMEM)] + [near] * (len(pieces) + 2),
        out_specs=near,
        scratch_shapes=[pltpu.VMEM((ROWS, pieces[0].shape[1]), BF16)],
        compiler_params=params(12),
        name="merge",
    )(y, *pieces, weight, bias)


def body(
    hidden_in,
    queries,
    keys,
    values,
    out_weight,
    out_bias,
    norm_gain,
    norm_bias,
    up_weight,
    up_bias,
    down_weight,
    down_bias,
    merge_weight,
    merge_bias,
    group_segments,
    owner_slots,
):
    heads = 4
    width = hidden_in.shape[1]
    request_total = owner_slots.shape[0]
    x = lax.axis_index("x")
    y = lax.axis_index("y")
    z = lax.axis_index("z")
    y_scalar = jnp.reshape(y, (1,)).astype(jnp.int32)

    swap = [(0, 1), (1, 0)]
    requests = jnp.arange(request_total, dtype=jnp.int32)
    key_parts = keys.T.reshape(heads, HD, ROWS)
    value_parts = values.T.reshape(heads, HD, ROWS)
    query_parts = queries.T.reshape(heads, HD, ROWS)
    marks = jnp.broadcast_to(jnp.repeat(group_segments, 4).astype(BF16), (heads, 8, ROWS))
    parts = jnp.concatenate([key_parts, value_parts, marks, query_parts], axis=1)
    def part_of(k):
        return lax.dynamic_slice_in_dim(parts, (x + k) & 3, 1, 0)

    own_parts = [part_of(0)] + [lax.ppermute(part_of(k), "x", ring(NX, k)) for k in range(1, NX)]
    own = jnp.concatenate(own_parts, axis=0)
    sent = own[:, :QUERY_AT]
    behind, ahead, far_a, far_b = [
        lax.ppermute(value, "z", ring(NZ, k))
        for value, k in ((sent, 1), (sent, NZ - 1), (sent[:2], 2), (sent[2:], 2))
    ]
    own_c = lax.ppermute(sent, "c", swap)
    place = jnp.stack([x, z]).astype(jnp.int32)
    state = attention_pass(place, own, [own, own_c], ((0, 0, 4), (1, 0, 4)), (), False)
    behind, ahead, far_a, far_b, state = lax.optimization_barrier(
        (behind, ahead, far_a, far_b, state)
    )
    out_weight, _ = lax.optimization_barrier((out_weight, state[0]))
    weights = [
        w.reshape(w.shape[0] // HD, HD, width) for w in (out_weight,) + shifted(out_weight)
    ]
    pieces = []
    for piece in (behind, ahead, far_a, far_b):
        pieces += [piece, lax.ppermute(piece, "c", swap)]
    layout = ((0, 0, 4), (1, 0, 4), (4, 0, 4), (5, 0, 4), (2, 0, 2), (3, 0, 2), (2, 2, 2), (3, 2, 2))
    attended, row_max = attention_pass(place, own, pieces, layout, state, True)
    row_segments = jnp.take(own[:, MARK_AT], (x - jnp.arange(NX)) & 3, axis=0).astype(jnp.int32)

    up_near, down_near = bring_near(row_max, up_weight, down_weight)
    attended = lax.all_to_all(attended.reshape(16, ROWS // NY, 128), ("y", "x"), 0, 0)
    mixed, normed = project(
        y_scalar, attended, weights, hidden_in, out_bias[None], norm_gain[None], norm_bias[None]
    )

    down = mlp((normed,) + shifted(normed), up_near, up_bias[None], down_near)
    back = [
        lax.ppermute(value, "y", ring(NY, NY - k))
        for value, k in ((down[1], 1), (down[4], 3), (down[2], 2), (down[3], 2))
    ]
    far = jnp.concatenate(back[2:], axis=0)
    state = mixed + down_bias + down[0]
    for value in (back[0], back[1], far):
        state = state + value.astype(F32)
    state_bf = state.astype(BF16)
    state_all = (state_bf,) + shifted(state_bf)

    member = row_segments[None] == requests[:, None, None]
    request_max = jnp.max(jnp.where(member, row_max[:, 0][None], NEGATIVE), axis=(1, 2))
    request_max = request_max * (HD**-0.5)
    own_groups = lax.dynamic_slice_in_dim(group_segments, y * (ROWS // 16), ROWS // 16)
    own_rows = jnp.repeat(own_groups, 4)
    mine = own_rows[None] == requests[:, None]
    own_counts = jnp.sum(mine.astype(F32), axis=1)
    row_slots = jnp.sum(jnp.where(mine, owner_slots[:, None], 0), axis=0)
    lane = lax.broadcasted_iota(jnp.int32, (CHUNKS, 128), 1)
    owner = lax.broadcasted_iota(jnp.int32, (CHUNKS, 128), 0)
    slot = 2 * owner + (lane & 1)
    facts = jnp.where(lane[None] < 4, request_max[:, None, None], own_counts[:, None, None])
    facts = jnp.sum(jnp.where(owner_slots[:, None, None] == slot[None], facts, 0.0), axis=0)
    squares = jnp.sum(state * state, axis=-1)
    sums = jnp.where(row_slots[:, None, None] == slot[None], squares[:, None, None], 0.0)
    sent = jnp.where(lane < 2, jnp.sum(sums, axis=0), facts)
    sent = jnp.broadcast_to(sent[None], (NY,) + sent.shape).reshape(NY * CHUNKS, 128)
    got = lax.all_to_all(sent, ("y", "x", "z", "c"), 0, 0, tiled=True)
    (merge_near,) = bring_near(got, merge_weight)
    merged_out = merge(y_scalar, state_all, merge_near, merge_bias[None])
    got = got.reshape(NY, NX, NZ * NC, 128)
    own_sums = jnp.sum(got[..., :2], axis=(0, 1, 2))
    own_counts = jnp.sum(got[..., 4:6], axis=(0, 1, 2))
    state_rms = jnp.sqrt(own_sums / (own_counts * width) + EPSILON)
    plane = lax.dynamic_index_in_dim(got[..., 2:4], y, 0, keepdims=False)
    logit_max = jnp.transpose(jnp.max(plane, axis=1))
    return (merged_out, state_rms, logit_max)


def solution(mesh):
    fine = Mesh(mesh.devices.reshape(NY, NX, NZ, NC), ("y", "x", "z", "c"))
    blk = ("x", "z", "c")
    in_specs = (
        P(blk, None),
        P(blk, "y"),
        P(blk, "y"),
        P(blk, "y"),
        P("y", None),
        P(),
        P(),
        P(),
        P(None, "y"),
        P("y"),
        P("y", None),
        P(),
        P(None, "y"),
        P("y"),
        P(blk),
        P(),
    )
    out_specs = (P(blk, "y"), P(blk), P(blk, "y"))
    return jax.shard_map(body, mesh=fine, in_specs=in_specs, out_specs=out_specs, check_vma=False)
```

```python
import functools

import jax
import jax.numpy as jnp
import numpy as np
from jax import lax
from jax.experimental import pallas as pl
from jax.experimental.pallas import tpu as pltpu
from jax.sharding import Mesh
from jax.sharding import PartitionSpec as P

HD = 88
NEGATIVE = -1e30
EPSILON = 1e-06
F32 = jnp.float32
BF16 = jnp.bfloat16

NY, NX, NZ, NC = 4, 4, 4, 2
ROWS = 384
CHUNKS = NX * NZ * NC
REQUESTS = 64
MARK_AT, QUERY_AT = 2 * HD, 2 * HD + 8
EXP2_SCALE = float(np.log2(np.e) / np.sqrt(HD))


def ring(size, shift):
    return [(i, (i + shift) % size) for i in range(size)]


def shifted(value):
    near = [lax.ppermute(value, "y", ring(NY, k)) for k in (1, 3)]
    half = value.shape[0] // 2
    far = [lax.ppermute(part, "y", ring(NY, 2)) for part in (value[:half], value[half:])]
    return near[0], far[0], far[1], near[1]


def in_hbm(value):
    return pltpu.with_memory_space_constraint(value, pltpu.HBM)


def params(mib):
    return pltpu.CompilerParams(vmem_limit_bytes=mib << 20)


def attention_kernel(first, last, per_x, layout, place_ref, *refs):
    count = len(layout)
    own, pieces, refs = refs[0], refs[1 : 1 + count], refs[1 + count :]
    if not first:
        top_in, mass_in, total_in = refs[:3]
        refs = refs[3:]
    if last:
        out_ref, top_ref, mass_at, total_at = refs[:4]
        refs = refs[4:]
    else:
        top_ref, mass_ref, total_ref = refs[:3]
        refs = refs[3:]
        mass_at, total_at = mass_ref.at[0], total_ref.at[0]
    top_at = top_ref.at[0]
    queries, marks, keys, values, key_marks, spread, s0, s1, p0, p1, ends, own_ends, sems = refs
    part = pl.program_id(0)
    x_here, z_here = place_ref[0], place_ref[1]
    steps = NX * per_x

    @pl.when(part == 0)
    def _():
        copies = [(own.at[:, pl.ds(QUERY_AT, HD)], queries), (own.at[:, pl.ds(MARK_AT, 8)], marks)]
        for piece, (slot, at, size) in zip(pieces, layout):
            at = pl.ds(at, size)
            copies.append((piece.at[:, pl.ds(0, HD)], keys.at[slot, at]))
            copies.append((piece.at[:, pl.ds(HD, HD)], values.at[slot, at]))
            copies.append((piece.at[:, pl.ds(MARK_AT, 8)], key_marks.at[slot, at]))
        copies = [pltpu.make_async_copy(*c, sems.at[i]) for i, c in enumerate(copies)]
        for copy in copies:
            copy.start()
        for copy in copies:
            copy.wait()
        for k in range(NX):
            mark = marks[k][:1].astype(F32)
            own_ends[k, 0] = jnp.min(mark)
            own_ends[k, 1] = jnp.max(mark)
            for pair in range(per_x):
                even = key_marks[2 * pair, k][:1].astype(F32)
                odd = key_marks[2 * pair + 1, k][:1].astype(F32)
                ends[pair, k, 0] = jnp.min(jnp.minimum(even, odd))
                ends[pair, k, 1] = jnp.max(jnp.maximum(even, odd))

    def locate(t):
        if per_x == 1:
            return 0, (x_here - t) & 3
        x_of = t // per_x
        z_of = t - x_of * per_x
        z_of = z_of + (z_of >= z_here).astype(jnp.int32)
        return ((z_here - z_of) & 3) - 1, (x_here - x_of) & 3

    here = (x_here - part) & 3
    mark = marks[here][:1].astype(F32)
    q_first, q_last = own_ends[here, 0], own_ends[here, 1]
    requests = lax.broadcasted_iota(jnp.int32, (REQUESTS, ROWS), 0).astype(F32)
    spread[...] = jnp.where(requests == mark, 1.0, 0.0).astype(BF16)
    low, high = jnp.int32(steps), jnp.int32(0)
    for t in range(steps):
        pair, at = locate(jnp.int32(t))
        active = (ends[pair, at, 1] >= q_first) & (ends[pair, at, 0] <= q_last)
        low = jnp.where(active & (low == steps), t, low)
        high = jnp.where(active, t + 1, high)

    if first:
        top_at[...] = jnp.full((1, ROWS), NEGATIVE, F32)
        mass_at[...] = jnp.zeros((1, ROWS), F32)
        total_at[...] = jnp.zeros((HD, ROWS), F32)
    else:
        top_at[...] = top_in[0]
        mass_at[...] = mass_in[0]
        total_at[...] = total_in[0]

    def both(a, b):
        return lax.dot_general(a, b, (((0,), (0,)), ((), ())), preferred_element_type=F32)

    def score(slot, at, scores):
        scores[...] = both(keys[slot, at], queries[here])

    def gather(slot, at, weights, factor):
        total_at[...] = total_at[...] * factor + jnp.dot(
            values[slot, at], weights[...], preferred_element_type=F32
        )

    def soften(slot, at, scores, weights, top, mass, mixed):
        s = scores[...]
        key_mark = key_marks[slot, at][:1].astype(F32)
        if mixed:
            key_spread = jnp.where(requests == key_mark, 1.0, 0.0).astype(BF16)
            s = jnp.where(both(key_spread, spread[...]) > 0.5, s, NEGATIVE)
            new_top = jnp.maximum(top, jnp.max(s, axis=0, keepdims=True))
            level = new_top
        else:
            has = mark == key_mark
            new_top = jnp.where(has, jnp.maximum(top, jnp.max(s, axis=0, keepdims=True)), top)
            level = jnp.where(has, new_top, -NEGATIVE)
        exponents = jnp.exp2((s - level) * EXP2_SCALE)
        factor = jnp.exp2((top - new_top) * EXP2_SCALE)
        weights[...] = exponents.astype(BF16)
        return new_top, mass * factor + jnp.sum(exponents, axis=0, keepdims=True), factor

    def step(t, pair, at, carried, mixed):
        top, mass, factor = carried
        old_pair, old_at = locate(jnp.maximum(t - 1, 0))
        new_pair, new_at = locate(jnp.minimum(t + 1, steps - 1))
        score(2 * pair + 1, at, s1)
        gather(2 * old_pair + 1, old_at, p1, factor)
        top, mass, factor = soften(2 * pair, at, s0, p0, top, mass, mixed)
        score(2 * new_pair, new_at, s0)
        gather(2 * pair, at, p0, factor)
        return soften(2 * pair + 1, at, s1, p1, top, mass, mixed)

    def one_pair(t, carried):
        pair, at = locate(t)
        return lax.cond(
            ends[pair, at, 0] == ends[pair, at, 1],
            lambda c: step(t, pair, at, c, False),
            lambda c: step(t, pair, at, c, True),
            carried,
        )

    @pl.when(high > low)
    def _():
        p1[...] = jnp.zeros_like(p1)
        pair, at = locate(low)
        score(2 * pair, at, s0)
        start = (top_at[...], mass_at[...], jnp.ones((1, ROWS), F32))
        top, mass, factor = lax.fori_loop(low, high, one_pair, start)
        pair, at = locate(high - 1)
        gather(2 * pair + 1, at, p1, factor)
        top_at[...] = top
        mass_at[...] = mass

    if last:
        attended = jnp.transpose(total_at[...] / mass_at[...]).astype(BF16)
        for y in range(NY):
            out_ref[y, 0, :, :HD] = attended[y * 96 : (y + 1) * 96]


def attention_pass(place, own, pieces, layout, state, last):
    per_x = 3 if state else 1
    slots = 2 * per_x
    whole = pl.BlockSpec(memory_space=pltpu.HBM)
    row = pl.BlockSpec((1, 1, ROWS), lambda i, t: (i, 0, 0))
    block = pl.BlockSpec((1, HD, ROWS), lambda i, t: (i, 0, 0))
    rows = jax.ShapeDtypeStruct((NX, 1, ROWS), F32)
    scratch = [
        pltpu.VMEM((NX, HD, ROWS), BF16),
        pltpu.VMEM((NX, 8, ROWS), BF16),
        pltpu.VMEM((slots, NX, HD, ROWS), BF16),
        pltpu.VMEM((slots, NX, HD, ROWS), BF16),
        pltpu.VMEM((slots, NX, 8, ROWS), BF16),
        pltpu.VMEM((REQUESTS, ROWS), BF16),
        pltpu.VMEM((ROWS, ROWS), F32),
        pltpu.VMEM((ROWS, ROWS), F32),
        pltpu.VMEM((ROWS, ROWS), BF16),
        pltpu.VMEM((ROWS, ROWS), BF16),
        pltpu.SMEM((per_x, NX, 2), F32),
        pltpu.SMEM((NX, 2), F32),
        pltpu.SemaphoreType.DMA((2 + 3 * len(layout),)),
    ]
    if last:
        out_shape = (jax.ShapeDtypeStruct((NY, NX, ROWS // NY, 128), BF16), rows)
        out_specs = (pl.BlockSpec((NY, 1, ROWS // NY, 128), lambda i, t: (0, i, 0, 0)), row)
        scratch = [pltpu.VMEM((1, ROWS), F32), pltpu.VMEM((HD, ROWS), F32)] + scratch
    else:
        out_shape = (rows, rows, jax.ShapeDtypeStruct((NX, HD, ROWS), F32))
        out_specs = (row, row, block)
    pairs = NX * NX * slots * ROWS * ROWS
    return pl.pallas_call(
        functools.partial(attention_kernel, not state, last, per_x, layout),
        out_shape=out_shape,
        grid_spec=pltpu.PrefetchScalarGridSpec(
            num_scalar_prefetch=1,
            grid=(NX,),
            in_specs=[whole] * (1 + len(pieces)) + [row, row, block][: len(state)],
            out_specs=out_specs,
            scratch_shapes=scratch,
        ),
        compiler_params=params(14),
        cost_estimate=pl.CostEstimate(
            flops=12 * pairs * HD, transcendentals=pairs, bytes_accessed=4 << 20
        ),
        name="attention_last" if last else "attention_pass",
    )(place, in_hbm(own), *[in_hbm(piece) for piece in pieces], *state)


def bring_near_kernel(after, *refs):
    count = len(refs) // 2
    sources, targets, sems = refs[:count], refs[count : 2 * count], refs[2 * count]
    copies = []
    for i, (source, target) in enumerate(zip(sources, targets)):
        size = source.shape[0] // 4
        for j in range(4):
            at = pl.ds(j * size, size)
            copies.append(pltpu.make_async_copy(source.at[at], target.at[at], sems.at[4 * i + j]))
    for copy in copies:
        copy.start()
    for copy in copies:
        copy.wait()


def bring_near(after, *weights):
    whole = pl.BlockSpec(memory_space=pltpu.HBM)
    return pl.pallas_call(
        bring_near_kernel,
        out_shape=[pltpu.VMEM(w.shape, w.dtype) for w in weights],
        in_specs=[pl.BlockSpec(memory_space=pl.ANY)] + [whole] * len(weights),
        out_specs=[pl.BlockSpec(memory_space=pltpu.VMEM)] * len(weights),
        scratch_shapes=[pltpu.SemaphoreType.DMA((4 * len(weights),))],
        compiler_params=params(8),
        cost_estimate=pl.CostEstimate(flops=0, transcendentals=0, bytes_accessed=10 << 20),
        name="bring_near",
    )(after, *[in_hbm(w) for w in weights])


def project_kernel(y_ref, att_ref, w0, w1, w2a, w2b, w3, hidden_ref, bias_ref, gain_ref, shift_ref,
                   mixed_ref, normed_ref):
    y = y_ref[0]
    mixed = hidden_ref[...].astype(F32) + bias_ref[...]
    for k, offset, w_ref in ((0, 0, w0), (1, 0, w1), (2, 0, w2a), (2, 2, w2b), (3, 0, w3)):
        base = ((y - k) & 3) * 4 + offset
        for i in range(w_ref.shape[0]):
            mixed = mixed + jnp.dot(att_ref[base + i, :, :HD], w_ref[i], preferred_element_type=F32)
    mixed_ref[...] = mixed
    mean = jnp.mean(mixed, axis=-1, keepdims=True)
    centered = mixed - mean
    var = jnp.mean(centered * centered, axis=-1, keepdims=True)
    normed = centered * lax.rsqrt(var + EPSILON) * gain_ref[...] + shift_ref[...]
    normed_ref[...] = normed.astype(BF16)


def project(y, attended, weights, hidden, bias, gain, shift):
    rows, width = ROWS // NY, hidden.shape[1]
    full = lambda *shape: pl.BlockSpec(shape, lambda i, t: (0,) * len(shape))
    return pl.pallas_call(
        project_kernel,
        out_shape=(
            jax.ShapeDtypeStruct((rows, width), F32),
            jax.ShapeDtypeStruct((rows, width), BF16),
        ),
        grid_spec=pltpu.PrefetchScalarGridSpec(
            num_scalar_prefetch=1,
            grid=(1,),
            in_specs=[full(16, rows, 128)]
            + [full(*w.shape) for w in weights]
            + [pl.BlockSpec((rows, width), lambda i, t: (t[0], 0))]
            + [full(1, width)] * 3,
            out_specs=(full(rows, width), full(rows, width)),
        ),
        compiler_params=params(16),
        name="project",
    )(y, attended, *weights, hidden, bias, gain, shift)


def mlp_kernel(x0, x1, x2a, x2b, x3, up_ref, bias_ref, down_ref, o0, o1, o2a, o2b, o3, rows, total):
    at = 0
    for x in (x0, x1, x2a, x2b, x3):
        rows[at : at + x.shape[0]] = x[...]
        at += x.shape[0]
    block = 384
    for step in range(up_ref.shape[1] // block):
        part = slice(step * block, (step + 1) * block)
        units = jnp.dot(rows[...], up_ref[:, part], preferred_element_type=F32) + bias_ref[:, part]
        units = 0.5 * units * (1.0 + lax.erf(units * float(np.sqrt(0.5))))
        down = jnp.dot(units.astype(BF16), down_ref[part], preferred_element_type=F32)
        total[...] = down if step == 0 else total[...] + down
    at = 0
    for o in (o0, o1, o2a, o2b, o3):
        o[...] = total[at : at + o.shape[0]].astype(o.dtype)
        at += o.shape[0]


def mlp(pieces, up_weight, up_bias, down_weight):
    width, hidden = up_weight.shape
    near = pl.BlockSpec(memory_space=pltpu.VMEM)
    return pl.pallas_call(
        mlp_kernel,
        out_shape=[
            jax.ShapeDtypeStruct(piece.shape, BF16 if k else F32) for k, piece in enumerate(pieces)
        ],
        in_specs=[near] * (len(pieces) + 3),
        out_specs=[near] * len(pieces),
        scratch_shapes=[pltpu.VMEM((ROWS, width), BF16), pltpu.VMEM((ROWS, width), F32)],
        compiler_params=params(12),
        cost_estimate=pl.CostEstimate(
            flops=4 * ROWS * width * hidden,
            transcendentals=ROWS * hidden,
            bytes_accessed=4 * width * hidden,
        ),
        name="mlp",
    )(*pieces, up_weight, up_bias, down_weight)


def merge_kernel(y_ref, x0, x1, x2a, x2b, x3, weight_ref, bias_ref, out_ref, rows):
    size = ROWS // NY
    groups = ROWS // 4
    width = rows.shape[1]
    at = 0
    for x in (x0, x1, x2a, x2b, x3):
        rows[at : at + x.shape[0]] = x[...]
        at += x.shape[0]
    at = lax.broadcasted_iota(jnp.int32, (groups, ROWS), 1)
    group = lax.broadcasted_iota(jnp.int32, (groups, ROWS), 0)
    piece = (at >= size).astype(jnp.int32) + (at >= 2 * size) + (at >= 3 * size)
    row = ((y_ref[0] - piece) & 3) * size + at - piece * size
    total = bias_ref[...]
    for member in range(4):
        pick = (row == 4 * group + member).astype(F32).astype(BF16)
        chosen = jnp.dot(pick, rows[...], preferred_element_type=F32).astype(BF16)
        weight = weight_ref[member * width : (member + 1) * width]
        total = total + jnp.dot(chosen, weight, preferred_element_type=F32)
    out_ref[...] = total.astype(BF16)


def merge(y, pieces, weight, bias):
    near = pl.BlockSpec(memory_space=pltpu.VMEM)
    return pl.pallas_call(
        merge_kernel,
        out_shape=jax.ShapeDtypeStruct((ROWS // 4, weight.shape[1]), BF16),
        in_specs=[pl.BlockSpec(memory_space=pltpu.SMEM)] + [near] * (len(pieces) + 2),
        out_specs=near,
        scratch_shapes=[pltpu.VMEM((ROWS, pieces[0].shape[1]), BF16)],
        compiler_params=params(12),
        name="merge",
    )(y, *pieces, weight, bias)


def body(
    hidden_in,
    queries,
    keys,
    values,
    out_weight,
    out_bias,
    norm_gain,
    norm_bias,
    up_weight,
    up_bias,
    down_weight,
    down_bias,
    merge_weight,
    merge_bias,
    group_segments,
    owner_slots,
):
    heads = 4
    width = hidden_in.shape[1]
    request_total = owner_slots.shape[0]
    x = lax.axis_index("x")
    y = lax.axis_index("y")
    z = lax.axis_index("z")
    y_scalar = jnp.reshape(y, (1,)).astype(jnp.int32)

    swap = [(0, 1), (1, 0)]
    requests = jnp.arange(request_total, dtype=jnp.int32)
    key_parts = keys.T.reshape(heads, HD, ROWS)
    value_parts = values.T.reshape(heads, HD, ROWS)
    query_parts = queries.T.reshape(heads, HD, ROWS)
    marks = jnp.broadcast_to(jnp.repeat(group_segments, 4).astype(BF16), (heads, 8, ROWS))
    parts = jnp.concatenate([key_parts, value_parts, marks, query_parts], axis=1)
    def part_of(k):
        return lax.dynamic_slice_in_dim(parts, (x + k) & 3, 1, 0)

    own_parts = [part_of(0)] + [lax.ppermute(part_of(k), "x", ring(NX, k)) for k in range(1, NX)]
    own = jnp.concatenate(own_parts, axis=0)
    sent = own[:, :QUERY_AT]
    behind, ahead, far_a, far_b = [
        lax.ppermute(value, "z", ring(NZ, k))
        for value, k in ((sent, 1), (sent, NZ - 1), (sent[:2], 2), (sent[2:], 2))
    ]
    own_c = lax.ppermute(sent, "c", swap)
    place = jnp.stack([x, z]).astype(jnp.int32)
    state = attention_pass(place, own, [own, own_c], ((0, 0, 4), (1, 0, 4)), (), False)
    behind, ahead, far_a, far_b, state = lax.optimization_barrier(
        (behind, ahead, far_a, far_b, state)
    )
    out_weight, _ = lax.optimization_barrier((out_weight, state[0]))
    weights = [
        w.reshape(w.shape[0] // HD, HD, width) for w in (out_weight,) + shifted(out_weight)
    ]
    pieces = []
    for piece in (behind, ahead, far_a, far_b):
        pieces += [piece, lax.ppermute(piece, "c", swap)]
    layout = ((0, 0, 4), (1, 0, 4), (4, 0, 4), (5, 0, 4), (2, 0, 2), (3, 0, 2), (2, 2, 2), (3, 2, 2))
    attended, row_max = attention_pass(place, own, pieces, layout, state, True)
    row_segments = jnp.take(own[:, MARK_AT], (x - jnp.arange(NX)) & 3, axis=0).astype(jnp.int32)

    up_near, down_near = bring_near(row_max, up_weight, down_weight)
    attended = lax.all_to_all(attended.reshape(16, ROWS // NY, 128), ("y", "x"), 0, 0)
    mixed, normed = project(
        y_scalar, attended, weights, hidden_in, out_bias[None], norm_gain[None], norm_bias[None]
    )

    down = mlp((normed,) + shifted(normed), up_near, up_bias[None], down_near)
    back = [
        lax.ppermute(value, "y", ring(NY, NY - k))
        for value, k in ((down[1], 1), (down[4], 3), (down[2], 2), (down[3], 2))
    ]
    far = jnp.concatenate(back[2:], axis=0)
    state = mixed + down_bias + down[0]
    for value in (back[0], back[1], far):
        state = state + value.astype(F32)
    state_bf = state.astype(BF16)
    state_all = (state_bf,) + shifted(state_bf)

    member = row_segments[None] == requests[:, None, None]
    request_max = jnp.max(jnp.where(member, row_max[:, 0][None], NEGATIVE), axis=(1, 2))
    request_max = request_max * (HD**-0.5)
    own_groups = lax.dynamic_slice_in_dim(group_segments, y * (ROWS // 16), ROWS // 16)
    own_rows = jnp.repeat(own_groups, 4)
    mine = own_rows[None] == requests[:, None]
    own_counts = jnp.sum(mine.astype(F32), axis=1)
    row_slots = jnp.sum(jnp.where(mine, owner_slots[:, None], 0), axis=0)
    lane = lax.broadcasted_iota(jnp.int32, (CHUNKS, 128), 1)
    owner = lax.broadcasted_iota(jnp.int32, (CHUNKS, 128), 0)
    slot = 2 * owner + (lane & 1)
    facts = jnp.where(lane[None] < 4, request_max[:, None, None], own_counts[:, None, None])
    facts = jnp.sum(jnp.where(owner_slots[:, None, None] == slot[None], facts, 0.0), axis=0)
    squares = jnp.sum(state * state, axis=-1)
    sums = jnp.where(row_slots[:, None, None] == slot[None], squares[:, None, None], 0.0)
    sent = jnp.where(lane < 2, jnp.sum(sums, axis=0), facts)
    sent = jnp.broadcast_to(sent[None], (NY,) + sent.shape).reshape(NY * CHUNKS, 128)
    got = lax.all_to_all(sent, ("y", "x", "z", "c"), 0, 0, tiled=True)
    (merge_near,) = bring_near(got, merge_weight)
    merged_out = merge(y_scalar, state_all, merge_near, merge_bias[None])
    got = got.reshape(NY, NX, NZ * NC, 128)
    own_sums = jnp.sum(got[..., :2], axis=(0, 1, 2))
    own_counts = jnp.sum(got[..., 4:6], axis=(0, 1, 2))
    state_rms = jnp.sqrt(own_sums / (own_counts * width) + EPSILON)
    plane = lax.dynamic_index_in_dim(got[..., 2:4], y, 0, keepdims=False)
    logit_max = jnp.transpose(jnp.max(plane, axis=1))
    return (merged_out, state_rms, logit_max)


def solution(mesh):
    fine = Mesh(mesh.devices.reshape(NY, NX, NZ, NC), ("y", "x", "z", "c"))
    blk = ("x", "z", "c")
    in_specs = (
        P(blk, None),
        P(blk, "y"),
        P(blk, "y"),
        P(blk, "y"),
        P("y", None),
        P(),
        P(),
        P(),
        P(None, "y"),
        P("y"),
        P("y", None),
        P(),
        P(None, "y"),
        P("y"),
        P(blk),
        P(),
    )
    out_specs = (P(blk, "y"), P(blk), P(blk, "y"))
    return jax.shard_map(body, mesh=fine, in_specs=in_specs, out_specs=out_specs, check_vma=False)
```

```python
import functools

import jax
import jax.numpy as jnp
import numpy as np
from jax import lax
from jax.experimental import pallas as pl
from jax.experimental.pallas import tpu as pltpu
from jax.sharding import Mesh
from jax.sharding import PartitionSpec as P

HD = 88
NEGATIVE = -1e30
EPSILON = 1e-06
F32 = jnp.float32
BF16 = jnp.bfloat16

NY, NX, NZ, NC = 4, 4, 4, 2
ROWS = 384
CHUNKS = NX * NZ * NC
REQUESTS = 64
MARK_AT, QUERY_AT = 2 * HD, 2 * HD + 8
EXP2_SCALE = float(np.log2(np.e) / np.sqrt(HD))


def ring(size, shift):
    return [(i, (i + shift) % size) for i in range(size)]


def shifted(value):
    near = [lax.ppermute(value, "y", ring(NY, k)) for k in (1, 3)]
    half = value.shape[0] // 2
    far = [lax.ppermute(part, "y", ring(NY, 2)) for part in (value[:half], value[half:])]
    return near[0], far[0], far[1], near[1]


def in_hbm(value):
    return pltpu.with_memory_space_constraint(value, pltpu.HBM)


def params(mib):
    return pltpu.CompilerParams(vmem_limit_bytes=mib << 20)


def attention_kernel(first, last, per_x, layout, place_ref, *refs):
    count = len(layout)
    own, pieces, refs = refs[0], refs[1 : 1 + count], refs[1 + count :]
    if not first:
        top_in, mass_in, total_in = refs[:3]
        refs = refs[3:]
    if last:
        out_ref, top_ref, mass_at, total_at = refs[:4]
        refs = refs[4:]
    else:
        top_ref, mass_ref, total_ref = refs[:3]
        refs = refs[3:]
        mass_at, total_at = mass_ref.at[0], total_ref.at[0]
    top_at = top_ref.at[0]
    queries, marks, keys, values, key_marks, spread, s0, s1, p0, p1, ends, own_ends, sems = refs
    part = pl.program_id(0)
    x_here, z_here = place_ref[0], place_ref[1]
    steps = NX * per_x

    @pl.when(part == 0)
    def _():
        copies = [(own.at[:, pl.ds(QUERY_AT, HD)], queries), (own.at[:, pl.ds(MARK_AT, 8)], marks)]
        for piece, (slot, at, size) in zip(pieces, layout):
            at = pl.ds(at, size)
            copies.append((piece.at[:, pl.ds(0, HD)], keys.at[slot, at]))
            copies.append((piece.at[:, pl.ds(HD, HD)], values.at[slot, at]))
            copies.append((piece.at[:, pl.ds(MARK_AT, 8)], key_marks.at[slot, at]))
        copies = [pltpu.make_async_copy(*c, sems.at[i]) for i, c in enumerate(copies)]
        for copy in copies:
            copy.start()
        for copy in copies:
            copy.wait()
        for k in range(NX):
            mark = marks[k][:1].astype(F32)
            own_ends[k, 0] = jnp.min(mark)
            own_ends[k, 1] = jnp.max(mark)
            for pair in range(per_x):
                even = key_marks[2 * pair, k][:1].astype(F32)
                odd = key_marks[2 * pair + 1, k][:1].astype(F32)
                ends[pair, k, 0] = jnp.min(jnp.minimum(even, odd))
                ends[pair, k, 1] = jnp.max(jnp.maximum(even, odd))

    def locate(t):
        if per_x == 1:
            return 0, (x_here - t) & 3
        x_of = t // per_x
        z_of = t - x_of * per_x
        z_of = z_of + (z_of >= z_here).astype(jnp.int32)
        return ((z_here - z_of) & 3) - 1, (x_here - x_of) & 3

    here = (x_here - part) & 3
    mark = marks[here][:1].astype(F32)
    q_first, q_last = own_ends[here, 0], own_ends[here, 1]
    requests = lax.broadcasted_iota(jnp.int32, (REQUESTS, ROWS), 0).astype(F32)
    spread[...] = jnp.where(requests == mark, 1.0, 0.0).astype(BF16)
    low, high = jnp.int32(steps), jnp.int32(0)
    for t in range(steps):
        pair, at = locate(jnp.int32(t))
        active = (ends[pair, at, 1] >= q_first) & (ends[pair, at, 0] <= q_last)
        low = jnp.where(active & (low == steps), t, low)
        high = jnp.where(active, t + 1, high)

    if first:
        top_at[...] = jnp.full((1, ROWS), NEGATIVE, F32)
        mass_at[...] = jnp.zeros((1, ROWS), F32)
        total_at[...] = jnp.zeros((HD, ROWS), F32)
    else:
        top_at[...] = top_in[0]
        mass_at[...] = mass_in[0]
        total_at[...] = total_in[0]

    def both(a, b):
        return lax.dot_general(a, b, (((0,), (0,)), ((), ())), preferred_element_type=F32)

    def score(slot, at, scores):
        scores[...] = both(keys[slot, at], queries[here])

    def gather(slot, at, weights, factor):
        total_at[...] = total_at[...] * factor + jnp.dot(
            values[slot, at], weights[...], preferred_element_type=F32
        )

    def soften(slot, at, scores, weights, top, mass, mixed):
        s = scores[...]
        key_mark = key_marks[slot, at][:1].astype(F32)
        if mixed:
            key_spread = jnp.where(requests == key_mark, 1.0, 0.0).astype(BF16)
            s = jnp.where(both(key_spread, spread[...]) > 0.5, s, NEGATIVE)
            new_top = jnp.maximum(top, jnp.max(s, axis=0, keepdims=True))
            level = new_top
        else:
            has = mark == key_mark
            new_top = jnp.where(has, jnp.maximum(top, jnp.max(s, axis=0, keepdims=True)), top)
            level = jnp.where(has, new_top, -NEGATIVE)
        exponents = jnp.exp2((s - level) * EXP2_SCALE)
        factor = jnp.exp2((top - new_top) * EXP2_SCALE)
        weights[...] = exponents.astype(BF16)
        return new_top, mass * factor + jnp.sum(exponents, axis=0, keepdims=True), factor

    def step(t, pair, at, carried, mixed):
        top, mass, factor = carried
        old_pair, old_at = locate(jnp.maximum(t - 1, 0))
        new_pair, new_at = locate(jnp.minimum(t + 1, steps - 1))
        score(2 * pair + 1, at, s1)
        gather(2 * old_pair + 1, old_at, p1, factor)
        top, mass, factor = soften(2 * pair, at, s0, p0, top, mass, mixed)
        score(2 * new_pair, new_at, s0)
        gather(2 * pair, at, p0, factor)
        return soften(2 * pair + 1, at, s1, p1, top, mass, mixed)

    def one_pair(t, carried):
        pair, at = locate(t)
        return lax.cond(
            ends[pair, at, 0] == ends[pair, at, 1],
            lambda c: step(t, pair, at, c, False),
            lambda c: step(t, pair, at, c, True),
            carried,
        )

    @pl.when(high > low)
    def _():
        p1[...] = jnp.zeros_like(p1)
        pair, at = locate(low)
        score(2 * pair, at, s0)
        start = (top_at[...], mass_at[...], jnp.ones((1, ROWS), F32))
        top, mass, factor = lax.fori_loop(low, high, one_pair, start)
        pair, at = locate(high - 1)
        gather(2 * pair + 1, at, p1, factor)
        top_at[...] = top
        mass_at[...] = mass

    if last:
        attended = jnp.transpose(total_at[...] / mass_at[...]).astype(BF16)
        for y in range(NY):
            out_ref[y, 0, :, :HD] = attended[y * 96 : (y + 1) * 96]


def attention_pass(place, own, pieces, layout, state, last):
    per_x = 3 if state else 1
    slots = 2 * per_x
    whole = pl.BlockSpec(memory_space=pltpu.HBM)
    row = pl.BlockSpec((1, 1, ROWS), lambda i, t: (i, 0, 0))
    block = pl.BlockSpec((1, HD, ROWS), lambda i, t: (i, 0, 0))
    rows = jax.ShapeDtypeStruct((NX, 1, ROWS), F32)
    scratch = [
        pltpu.VMEM((NX, HD, ROWS), BF16),
        pltpu.VMEM((NX, 8, ROWS), BF16),
        pltpu.VMEM((slots, NX, HD, ROWS), BF16),
        pltpu.VMEM((slots, NX, HD, ROWS), BF16),
        pltpu.VMEM((slots, NX, 8, ROWS), BF16),
        pltpu.VMEM((REQUESTS, ROWS), BF16),
        pltpu.VMEM((ROWS, ROWS), F32),
        pltpu.VMEM((ROWS, ROWS), F32),
        pltpu.VMEM((ROWS, ROWS), BF16),
        pltpu.VMEM((ROWS, ROWS), BF16),
        pltpu.SMEM((per_x, NX, 2), F32),
        pltpu.SMEM((NX, 2), F32),
        pltpu.SemaphoreType.DMA((2 + 3 * len(layout),)),
    ]
    if last:
        out_shape = (jax.ShapeDtypeStruct((NY, NX, ROWS // NY, 128), BF16), rows)
        out_specs = (pl.BlockSpec((NY, 1, ROWS // NY, 128), lambda i, t: (0, i, 0, 0)), row)
        scratch = [pltpu.VMEM((1, ROWS), F32), pltpu.VMEM((HD, ROWS), F32)] + scratch
    else:
        out_shape = (rows, rows, jax.ShapeDtypeStruct((NX, HD, ROWS), F32))
        out_specs = (row, row, block)
    pairs = NX * NX * slots * ROWS * ROWS
    return pl.pallas_call(
        functools.partial(attention_kernel, not state, last, per_x, layout),
        out_shape=out_shape,
        grid_spec=pltpu.PrefetchScalarGridSpec(
            num_scalar_prefetch=1,
            grid=(NX,),
            in_specs=[whole] * (1 + len(pieces)) + [row, row, block][: len(state)],
            out_specs=out_specs,
            scratch_shapes=scratch,
        ),
        compiler_params=params(14),
        cost_estimate=pl.CostEstimate(
            flops=12 * pairs * HD, transcendentals=pairs, bytes_accessed=4 << 20
        ),
        name="attention_last" if last else "attention_pass",
    )(place, in_hbm(own), *[in_hbm(piece) for piece in pieces], *state)


def bring_near_kernel(after, *refs):
    count = len(refs) // 2
    sources, targets, sems = refs[:count], refs[count : 2 * count], refs[2 * count]
    copies = []
    for i, (source, target) in enumerate(zip(sources, targets)):
        size = source.shape[0] // 4
        for j in range(4):
            at = pl.ds(j * size, size)
            copies.append(pltpu.make_async_copy(source.at[at], target.at[at], sems.at[4 * i + j]))
    for copy in copies:
        copy.start()
    for copy in copies:
        copy.wait()


def bring_near(after, *weights):
    whole = pl.BlockSpec(memory_space=pltpu.HBM)
    return pl.pallas_call(
        bring_near_kernel,
        out_shape=[pltpu.VMEM(w.shape, w.dtype) for w in weights],
        in_specs=[pl.BlockSpec(memory_space=pl.ANY)] + [whole] * len(weights),
        out_specs=[pl.BlockSpec(memory_space=pltpu.VMEM)] * len(weights),
        scratch_shapes=[pltpu.SemaphoreType.DMA((4 * len(weights),))],
        compiler_params=params(8),
        cost_estimate=pl.CostEstimate(flops=0, transcendentals=0, bytes_accessed=10 << 20),
        name="bring_near",
    )(after, *[in_hbm(w) for w in weights])


def project_kernel(y_ref, att_ref, w0, w1, w2a, w2b, w3, hidden_ref, bias_ref, gain_ref, shift_ref,
                   mixed_ref, normed_ref):
    y = y_ref[0]
    mixed = hidden_ref[...].astype(F32) + bias_ref[...]
    for k, offset, w_ref in ((0, 0, w0), (1, 0, w1), (2, 0, w2a), (2, 2, w2b), (3, 0, w3)):
        base = ((y - k) & 3) * 4 + offset
        for i in range(w_ref.shape[0]):
            mixed = mixed + jnp.dot(att_ref[base + i, :, :HD], w_ref[i], preferred_element_type=F32)
    mixed_ref[...] = mixed
    mean = jnp.mean(mixed, axis=-1, keepdims=True)
    centered = mixed - mean
    var = jnp.mean(centered * centered, axis=-1, keepdims=True)
    normed = centered * lax.rsqrt(var + EPSILON) * gain_ref[...] + shift_ref[...]
    normed_ref[...] = normed.astype(BF16)


def project(y, attended, weights, hidden, bias, gain, shift):
    rows, width = ROWS // NY, hidden.shape[1]
    full = lambda *shape: pl.BlockSpec(shape, lambda i, t: (0,) * len(shape))
    return pl.pallas_call(
        project_kernel,
        out_shape=(
            jax.ShapeDtypeStruct((rows, width), F32),
            jax.ShapeDtypeStruct((rows, width), BF16),
        ),
        grid_spec=pltpu.PrefetchScalarGridSpec(
            num_scalar_prefetch=1,
            grid=(1,),
            in_specs=[full(16, rows, 128)]
            + [full(*w.shape) for w in weights]
            + [pl.BlockSpec((rows, width), lambda i, t: (t[0], 0))]
            + [full(1, width)] * 3,
            out_specs=(full(rows, width), full(rows, width)),
        ),
        compiler_params=params(16),
        name="project",
    )(y, attended, *weights, hidden, bias, gain, shift)


def mlp_kernel(x0, x1, x2a, x2b, x3, up_ref, bias_ref, down_ref, o0, o1, o2a, o2b, o3, rows, total):
    at = 0
    for x in (x0, x1, x2a, x2b, x3):
        rows[at : at + x.shape[0]] = x[...]
        at += x.shape[0]
    block = 384
    for step in range(up_ref.shape[1] // block):
        part = slice(step * block, (step + 1) * block)
        units = jnp.dot(rows[...], up_ref[:, part], preferred_element_type=F32) + bias_ref[:, part]
        units = 0.5 * units * (1.0 + lax.erf(units * float(np.sqrt(0.5))))
        down = jnp.dot(units.astype(BF16), down_ref[part], preferred_element_type=F32)
        total[...] = down if step == 0 else total[...] + down
    at = 0
    for o in (o0, o1, o2a, o2b, o3):
        o[...] = total[at : at + o.shape[0]].astype(o.dtype)
        at += o.shape[0]


def mlp(pieces, up_weight, up_bias, down_weight):
    width, hidden = up_weight.shape
    near = pl.BlockSpec(memory_space=pltpu.VMEM)
    return pl.pallas_call(
        mlp_kernel,
        out_shape=[
            jax.ShapeDtypeStruct(piece.shape, BF16 if k else F32) for k, piece in enumerate(pieces)
        ],
        in_specs=[near] * (len(pieces) + 3),
        out_specs=[near] * len(pieces),
        scratch_shapes=[pltpu.VMEM((ROWS, width), BF16), pltpu.VMEM((ROWS, width), F32)],
        compiler_params=params(12),
        cost_estimate=pl.CostEstimate(
            flops=4 * ROWS * width * hidden,
            transcendentals=ROWS * hidden,
            bytes_accessed=4 * width * hidden,
        ),
        name="mlp",
    )(*pieces, up_weight, up_bias, down_weight)


def merge_kernel(y_ref, x0, x1, x2a, x2b, x3, weight_ref, bias_ref, out_ref, rows):
    size = ROWS // NY
    groups = ROWS // 4
    width = rows.shape[1]
    at = 0
    for x in (x0, x1, x2a, x2b, x3):
        rows[at : at + x.shape[0]] = x[...]
        at += x.shape[0]
    at = lax.broadcasted_iota(jnp.int32, (groups, ROWS), 1)
    group = lax.broadcasted_iota(jnp.int32, (groups, ROWS), 0)
    piece = (at >= size).astype(jnp.int32) + (at >= 2 * size) + (at >= 3 * size)
    row = ((y_ref[0] - piece) & 3) * size + at - piece * size
    total = bias_ref[...]
    for member in range(4):
        pick = (row == 4 * group + member).astype(F32).astype(BF16)
        chosen = jnp.dot(pick, rows[...], preferred_element_type=F32).astype(BF16)
        weight = weight_ref[member * width : (member + 1) * width]
        total = total + jnp.dot(chosen, weight, preferred_element_type=F32)
    out_ref[...] = total.astype(BF16)


def merge(y, pieces, weight, bias):
    near = pl.BlockSpec(memory_space=pltpu.VMEM)
    return pl.pallas_call(
        merge_kernel,
        out_shape=jax.ShapeDtypeStruct((ROWS // 4, weight.shape[1]), BF16),
        in_specs=[pl.BlockSpec(memory_space=pltpu.SMEM)] + [near] * (len(pieces) + 2),
        out_specs=near,
        scratch_shapes=[pltpu.VMEM((ROWS, pieces[0].shape[1]), BF16)],
        compiler_params=params(12),
        name="merge",
    )(y, *pieces, weight, bias)


def body(
    hidden_in,
    queries,
    keys,
    values,
    out_weight,
    out_bias,
    norm_gain,
    norm_bias,
    up_weight,
    up_bias,
    down_weight,
    down_bias,
    merge_weight,
    merge_bias,
    group_segments,
    owner_slots,
):
    heads = 4
    width = hidden_in.shape[1]
    request_total = owner_slots.shape[0]
    x = lax.axis_index("x")
    y = lax.axis_index("y")
    z = lax.axis_index("z")
    y_scalar = jnp.reshape(y, (1,)).astype(jnp.int32)

    swap = [(0, 1), (1, 0)]
    requests = jnp.arange(request_total, dtype=jnp.int32)
    key_parts = keys.T.reshape(heads, HD, ROWS)
    value_parts = values.T.reshape(heads, HD, ROWS)
    query_parts = queries.T.reshape(heads, HD, ROWS)
    marks = jnp.broadcast_to(jnp.repeat(group_segments, 4).astype(BF16), (heads, 8, ROWS))
    parts = jnp.concatenate([key_parts, value_parts, marks, query_parts], axis=1)
    def part_of(k):
        return lax.dynamic_slice_in_dim(parts, (x + k) & 3, 1, 0)

    own_parts = [part_of(0)] + [lax.ppermute(part_of(k), "x", ring(NX, k)) for k in range(1, NX)]
    own = jnp.concatenate(own_parts, axis=0)
    sent = own[:, :QUERY_AT]
    behind = lax.ppermute(sent, "z", ring(NZ, 1))
    ahead = lax.ppermute(sent, "z", ring(NZ, NZ - 1))
    own_c = lax.ppermute(sent, "c", swap)
    place = jnp.stack([x, z]).astype(jnp.int32)
    state = attention_pass(place, own, [own, own_c], ((0, 0, 4), (1, 0, 4)), (), False)
    behind, ahead, state = lax.optimization_barrier((behind, ahead, state))
    far_a = lax.ppermute(behind[:2], "z", ring(NZ, 1))
    far_b = lax.ppermute(ahead[2:], "z", ring(NZ, NZ - 1))
    pieces = []
    for piece in (behind, ahead, far_a, far_b):
        pieces += [piece, lax.ppermute(piece, "c", swap)]
    weight, _ = lax.optimization_barrier((out_weight, (far_a, far_b)))
    weights = [
        w.reshape(w.shape[0] // HD, HD, width) for w in (out_weight,) + shifted(weight)
    ]
    layout = ((0, 0, 4), (1, 0, 4), (4, 0, 4), (5, 0, 4), (2, 0, 2), (3, 0, 2), (2, 2, 2), (3, 2, 2))
    attended, row_max = attention_pass(place, own, pieces, layout, state, True)
    row_segments = jnp.take(own[:, MARK_AT], (x - jnp.arange(NX)) & 3, axis=0).astype(jnp.int32)

    up_near, down_near = bring_near(row_max, up_weight, down_weight)
    attended = lax.all_to_all(attended.reshape(16, ROWS // NY, 128), ("y", "x"), 0, 0)
    mixed, normed = project(
        y_scalar, attended, weights, hidden_in, out_bias[None], norm_gain[None], norm_bias[None]
    )

    down = mlp((normed,) + shifted(normed), up_near, up_bias[None], down_near)
    back = [
        lax.ppermute(value, "y", ring(NY, NY - k))
        for value, k in ((down[1], 1), (down[4], 3), (down[2], 2), (down[3], 2))
    ]
    far = jnp.concatenate(back[2:], axis=0)
    state = mixed + down_bias + down[0]
    for value in (back[0], back[1], far):
        state = state + value.astype(F32)
    state_bf = state.astype(BF16)
    state_all = (state_bf,) + shifted(state_bf)

    member = row_segments[None] == requests[:, None, None]
    request_max = jnp.max(jnp.where(member, row_max[:, 0][None], NEGATIVE), axis=(1, 2))
    request_max = request_max * (HD**-0.5)
    own_groups = lax.dynamic_slice_in_dim(group_segments, y * (ROWS // 16), ROWS // 16)
    own_rows = jnp.repeat(own_groups, 4)
    mine = own_rows[None] == requests[:, None]
    own_counts = jnp.sum(mine.astype(F32), axis=1)
    row_slots = jnp.sum(jnp.where(mine, owner_slots[:, None], 0), axis=0)
    lane = lax.broadcasted_iota(jnp.int32, (CHUNKS, 128), 1)
    owner = lax.broadcasted_iota(jnp.int32, (CHUNKS, 128), 0)
    slot = 2 * owner + (lane & 1)
    facts = jnp.where(lane[None] < 4, request_max[:, None, None], own_counts[:, None, None])
    facts = jnp.sum(jnp.where(owner_slots[:, None, None] == slot[None], facts, 0.0), axis=0)
    squares = jnp.sum(state * state, axis=-1)
    sums = jnp.where(row_slots[:, None, None] == slot[None], squares[:, None, None], 0.0)
    sent = jnp.where(lane < 2, jnp.sum(sums, axis=0), facts)
    sent = jnp.broadcast_to(sent[None], (NY,) + sent.shape).reshape(NY * CHUNKS, 128)
    got = lax.all_to_all(sent, ("y", "x", "z", "c"), 0, 0, tiled=True)
    (merge_near,) = bring_near(got, merge_weight)
    merged_out = merge(y_scalar, state_all, merge_near, merge_bias[None])
    got = got.reshape(NY, NX, NZ * NC, 128)
    own_sums = jnp.sum(got[..., :2], axis=(0, 1, 2))
    own_counts = jnp.sum(got[..., 4:6], axis=(0, 1, 2))
    state_rms = jnp.sqrt(own_sums / (own_counts * width) + EPSILON)
    plane = lax.dynamic_index_in_dim(got[..., 2:4], y, 0, keepdims=False)
    logit_max = jnp.transpose(jnp.max(plane, axis=1))
    return (merged_out, state_rms, logit_max)


def solution(mesh):
    fine = Mesh(mesh.devices.reshape(NY, NX, NZ, NC), ("y", "x", "z", "c"))
    blk = ("x", "z", "c")
    in_specs = (
        P(blk, None),
        P(blk, "y"),
        P(blk, "y"),
        P(blk, "y"),
        P("y", None),
        P(),
        P(),
        P(),
        P(None, "y"),
        P("y"),
        P("y", None),
        P(),
        P(None, "y"),
        P("y"),
        P(blk),
        P(),
    )
    out_specs = (P(blk, "y"), P(blk), P(blk, "y"))
    return jax.shard_map(body, mesh=fine, in_specs=in_specs, out_specs=out_specs, check_vma=False)
```
